32 devices in a mesh: section: 4 (over x, core), ha: 2 (over y), wa: 4 (over z).
Axes of the slice: x: 2, y: 2, z: 4, core: 2. Of those that a mesh axis runs over, the one named last changes fastest.
Arguments:
- queries: bfloat16 [4, 4, 4, 8, 16, 2560], P('section', None, 'ha', 'wa'), may hold values from -28 to 28
- keys_values: bfloat16 [2, 4, 4, 4, 8, 16, 2560], P(None, 'section', None, 'ha', 'wa'), may hold values from -28 to 28
- grad_out: bfloat16 [4, 4, 4, 8, 16, 2560], P('section', None, 'ha', 'wa'), may hold values from -6 to 6
- time_start: int32 [4, 4, 8], P(None, 'ha', 'wa'), may hold values from 0 to 1, as said below
Outputs:
- grad_qkv: bfloat16 [3, 4, 4, 4, 8, 16, 2560], P(None, 'section', None, 'ha', 'wa')
The draws below stay inside these ranges and needn't reach their ends.
Inputs may be any that keep to these rules, and one draw needn't show every extreme that they name: Each tile's window begins at most two tiles before the tile and never after it: max(0, t - 2) <= time_start[t, h, w] <= min(t, 1) for time index t.
All inputs are finite; a program needn't handle non-finite values.
Results may differ from the reference program's by a relative error of at most 0.012.
Values may be sent and summed in bfloat16 or wider, within the bound.
A program may use at most 192 MiB of HBM per device.

```python
import jax
import jax.numpy as jnp
from jax import lax

HEADS = 20
HEAD_DIM = 128
GT = 4
HT = 2
WT = 2
SECTIONS = 4
GH = 4
GW = 8
TILE_TOK = 16
CHANNELS = 2560
N_HA = 2
N_WA = 4


def drawn_draw(key):
    base = jax.random.fold_in(key, 71)
    pair_shape = (2, SECTIONS, GT, GH, GW, TILE_TOK, CHANNELS)
    pairs = jnp.clip(jax.random.normal(jax.random.fold_in(base, 1), pair_shape, jnp.float32), -6.0, 6.0)
    queries = jnp.clip(jax.random.normal(jax.random.fold_in(base, 2), pair_shape[1:], jnp.float32), -6.0, 6.0)
    return (queries, pairs)


def draw_queries(key, part):
    return drawn_draw(key)[0].astype(jnp.bfloat16)


def draw_keys_values(key, part):
    return drawn_draw(key)[1].astype(jnp.bfloat16)


def draw_time_start(key, part):
    shifts = jax.random.randint(jax.random.fold_in(key, 5), (GT, GH, GW), 0, 3)
    tiles = jnp.arange(GT, dtype=jnp.int32)[:, None, None]
    return jnp.clip(tiles - shifts, 0, GT - 3).astype(jnp.int32)


def block_levels(own_key, shape, split, low, largest):
    factor_of = 1.0
    for axis_at, blocks in split:
        steps = jax.random.uniform(jax.random.fold_in(jax.random.fold_in(own_key, 6), axis_at), (blocks,), jnp.float32, low / len(split), largest / len(split))
        factor_of = factor_of * jnp.repeat(jnp.exp(steps), shape[axis_at] // blocks).reshape((-1,) + (1,) * (len(shape) - 1 - axis_at))
    return factor_of


def centred(stream_key, dims, deviation, limit, shards=(), held_as=jnp.bfloat16):
    loudness = block_levels(stream_key, dims, shards, -0.22, 0.18) if shards else 1.0
    array = jax.random.normal(stream_key, dims, jnp.float32) * deviation * loudness
    return jnp.minimum(jnp.maximum(array, -limit), limit).astype(held_as)


def setup_inputs(seed: int = 0) -> dict:
    splits = jax.random.split(jax.random.key(seed), 5)
    queries = draw_queries(jax.random.fold_in(splits[4], 71), 0)
    keys_values = draw_keys_values(jax.random.fold_in(splits[4], 71), 0)
    grad_out = centred(splits[2], (SECTIONS, GT, GH, GW, TILE_TOK, CHANNELS), 1.0, 6.0, ((0, 4), (2, 2), (3, 4)))
    time_start = draw_time_start(jax.random.fold_in(splits[4], 71), 0)
    return {"queries": queries, "keys_values": keys_values, "grad_out": grad_out, "time_start": time_start}


def tile_grads(query_block, pair_block, grad_block, starts, tile_tok):
    scale_factor = HEAD_DIM ** -0.5
    query_full = query_block.astype(jnp.float32)
    key_part = pair_block[0].astype(jnp.float32)
    value_part = pair_block[1].astype(jnp.float32)
    grad_full = grad_block.astype(jnp.float32)
    scores = jnp.einsum("qhd,khd->hqk", query_full, key_part) * scale_factor
    key_tile = jnp.arange(key_part.shape[0], dtype=jnp.int32) // (9 * tile_tok)
    window_low = jnp.repeat(starts.astype(jnp.int32), tile_tok)
    inside = (key_tile[None, :] >= window_low[:, None]) & (key_tile[None, :] < window_low[:, None] + 3)
    scores = jnp.where(inside[None], scores, -jnp.inf)
    maximum = jnp.max(scores, axis=-1, keepdims=True)
    weights = jnp.exp(scores - maximum)
    softmax_out = weights / jnp.sum(weights, axis=-1, keepdims=True)
    weights_low = softmax_out.astype(jnp.bfloat16).astype(jnp.float32)
    grad_probs = jnp.einsum("qhd,khd->hqk", grad_full, value_part)
    row_delta = jnp.sum(softmax_out * grad_probs, axis=-1, keepdims=True)
    grad_scores = (softmax_out * (grad_probs - row_delta)).astype(jnp.bfloat16).astype(jnp.float32)
    query_grad = jnp.einsum("hqk,khd->qhd", grad_scores, key_part) * scale_factor
    key_grad = jnp.einsum("hqk,qhd->khd", grad_scores, query_full) * scale_factor
    value_grad = jnp.einsum("hqk,qhd->khd", weights_low, grad_full)
    return query_grad, jnp.stack([key_grad, value_grad])


def reference(queries, keys_values, grad_out, time_start):
    tile_count = GT * TILE_TOK
    interior = jnp.zeros((HT + 2, WT + 2), dtype=bool).at[1:HT + 1, 1:WT + 1].set(True)

    def section_grads(operands):
        section_queries, section_pairs, section_grads_out = operands
        total = jnp.zeros((2, GT, GH + 2, GW + 2, TILE_TOK, CHANNELS), jnp.float32)
        query_total = jnp.zeros((GT, GH, GW, TILE_TOK, CHANNELS), jnp.bfloat16)
        for dev_row in range(N_HA):
            for dev_col in range(N_WA):
                partial_value = jnp.zeros((2, GT, HT + 2, WT + 2, TILE_TOK, CHANNELS), jnp.float32)
                for tile_row in range(HT):
                    for tile_col in range(WT):
                        glob_row = dev_row * HT + tile_row
                        glob_col = dev_col * WT + tile_col
                        top_start = min(max(glob_row - 1, 0), GH - 3)
                        left_start = min(max(glob_col - 1, 0), GW - 3)
                        window = section_pairs[:, :, top_start:top_start + 3, left_start:left_start + 3]
                        pair_block = window.reshape(2, tile_count * 9, HEADS, HEAD_DIM)
                        query_block = section_queries[:, glob_row, glob_col].reshape(tile_count, HEADS, HEAD_DIM)
                        grad_block = section_grads_out[:, glob_row, glob_col].reshape(tile_count, HEADS, HEAD_DIM)
                        query_grad, pair_grad = tile_grads(query_block, pair_block, grad_block, time_start[:, glob_row, glob_col], TILE_TOK)
                        query_total = query_total.at[:, glob_row, glob_col].set(query_grad.reshape(GT, TILE_TOK, CHANNELS).astype(jnp.bfloat16))
                        ext_row = top_start - dev_row * HT + 1
                        ext_col = left_start - dev_col * WT + 1
                        partial_value = partial_value.at[:, :, ext_row:ext_row + 3, ext_col:ext_col + 3].add(pair_grad.reshape(2, GT, 3, 3, TILE_TOK, CHANNELS))
                rim_values = lax.optimization_barrier(partial_value.astype(jnp.bfloat16)).astype(jnp.float32)
                mixed = jnp.where(interior[None, None, :, :, None, None], partial_value, rim_values)
                total = total.at[:, :, dev_row * HT:dev_row * HT + HT + 2, dev_col * WT:dev_col * WT + WT + 2].add(mixed)
        pair_total = total[:, :, 1:GH + 1, 1:GW + 1].astype(jnp.bfloat16)
        return jnp.concatenate([query_total[None], pair_total], axis=0)

    per_section = lax.map(section_grads, (queries, jnp.moveaxis(keys_values, 1, 0), grad_out))
    shifted = jnp.roll(per_section, -1, axis=0)
    return jnp.moveaxis(shifted, 0, 1)
```

```python
import functools

import jax
import jax.numpy as jnp
from jax import lax
from jax.experimental import pallas as pl
from jax.experimental.pallas import tpu as pltpu
from jax.sharding import PartitionSpec as P

HEAD_DIM = 128
HEADS_PER_CHUNK = 1
MESH = pl.DeviceIdType.MESH
F32 = jnp.float32
BF16 = jnp.bfloat16

Y_KV, Z_Q, Z_GO, EXT, CORNER, STAT, DQ, EXT_PART, Y_PART, OUT_Q, OUT_KV, KINDS = 0, 1, 3, 5, 6, 7, 9, 11, 12, 13, 14, 15

AHEAD = 4
CORNERS_AHEAD = 2
STAT_LAG = 2
FOLD_LAG = 4
OUT_LAG = 6
LOW = -1e30


def dot(a, b, contract):
    return lax.dot_general(a, b, ((contract[0], contract[1]), ((), ())), preferred_element_type=F32)


def merge(top, lse, mean, lse_other, mean_other):
    most = jnp.maximum(lse, lse_other)
    w, w_other = jnp.exp(lse - most), jnp.exp(lse_other - most)
    inv = 1.0 / (w + w_other)
    return jnp.exp(top - most) * inv, (w * mean + w_other * mean_other) * inv


def kernel(sizes, starts, q_in, kv_in, go_in, out, q, go, kx, qz, load_sem, first_send, first_recv, first_sem, bias,
           bias_z, e_own, dp_own, st_own, e_z, dp_z, st_z, stat_send, stat_recv, acc, dqa, dqz_send, dqz_recv,
           pz_send, pz_recv, py_send, py_recv, dq, dkv, send_sem, recv_sem):
    n_sec, n_ha, n_wa, chunks, width = sizes
    grid_t, rows, cols, tok, _ = q.shape
    per_col = grid_t * rows * tok
    per_key = grid_t * (rows + 1) * tok
    slots = e_own.shape[0]
    sec, ha, wa = lax.axis_index("section"), lax.axis_index("ha"), lax.axis_index("wa")
    before = lax.rem(sec + n_sec - 1, n_sec)
    after = lax.rem(sec + 1, n_sec)
    other = 1 - ha
    edge = other * (rows - 1)
    has = (wa > 0, wa < n_wa - 1)
    peer = (wa - 1, wa + 1)
    near = (0, cols - 1)
    rim = (wa == 0) | (wa == n_wa - 1)
    by_rim = (wa == 1, wa == n_wa - 2)
    scale = HEAD_DIM ** (-0.5)

    loads = [pltpu.make_async_copy(src, dst, load_sem.at[n]) for n, (src, dst) in enumerate(
        ((q_in, q), (kv_in, kx.at[:, :, 0:rows, 0:cols]), (go_in, go)))]
    barrier = pltpu.get_barrier_semaphore()
    pl.semaphore_signal(barrier, inc=1, device_id=(before, ha, wa), device_id_type=MESH)
    pl.semaphore_signal(barrier, inc=1, device_id=(after, ha, wa), device_id_type=MESH)
    pl.semaphore_signal(barrier, inc=1, device_id=(sec, other, wa), device_id_type=MESH)
    for side in (0, 1):
        @pl.when(has[side])
        def _():
            pl.semaphore_signal(barrier, inc=1, device_id=(sec, ha, peer[side]), device_id_type=MESH)
    pl.semaphore_wait(barrier, 3 + jnp.minimum(wa, 1) + jnp.minimum(n_wa - 1 - wa, 1))

    def keys_move(c):
        return (lax.rem(c, 2) == 1) & (c < chunks - 2)

    def lanes(c):
        return pl.ds(pl.multiple_of(c * width, width), width)

    def channels(c, j):
        return pl.ds(pl.multiple_of(c * width + j * HEAD_DIM, HEAD_DIM), HEAD_DIM)

    def remote(src, dst, sent, arrived, c, device):
        return pltpu.make_async_remote_copy(
            src_ref=src, dst_ref=dst, send_sem=send_sem.at[sent, c], recv_sem=recv_sem.at[arrived, c],
            device_id=device, device_id_type=MESH)

    def y_kv(c):
        return remote(kv_in.at[:, :, edge, :, :, lanes(c)], kx.at[:, :, rows, 0:cols, :, lanes(c)],
                      Y_KV, Y_KV, c, (sec, other, wa))

    class Pair:
        def __init__(self, *copies):
            self.copies = copies

        def start(self):
            for copy in self.copies:
                copy.start()

        def wait_send(self):
            for copy in self.copies:
                copy.wait_send()

        def wait_recv(self):
            for copy in self.copies:
                copy.wait_recv()

    def z_q(side, c, both):
        col = near[side]
        at = slice(0, cols) if both else slice(col, col + 1)
        return Pair(*(
            remote(src.at[:, :, at, :, lanes(c)], qz.at[1 - side, n, :, :, at, :, lanes(c)],
                   kind + side, kind + 1 - side, c, (sec, ha, peer[side]))
            for n, (src, kind) in enumerate(((q_in, Z_Q), (go_in, Z_GO)))))

    def ext(side, c):
        return remote(kv_in.at[:, :, :, near[side], :, lanes(c)], kx.at[:, :, 0:rows, cols, :, lanes(c)],
                      EXT, EXT, c, (sec, ha, peer[side]))

    def corner(side, c):
        return remote(kx.at[:, :, rows, near[side], :, lanes(c)], kx.at[:, :, rows, cols, :, lanes(c)],
                      CORNER, CORNER, c, (sec, ha, peer[side]))

    def stat(side, c, both):
        at = slice(0, per_col * (cols if both else 1))
        return remote(stat_send.at[side, c, :, at], stat_recv.at[1 - side, c, :, at],
                      STAT + side, STAT + 1 - side, c, (sec, ha, peer[side]))

    def dq_back(side, c, both):
        col = near[1 - side]
        at = slice(0, cols) if both else slice(col, col + 1)
        return remote(dqz_send.at[side, :, :, at, :, lanes(c)], dqz_recv.at[1 - side, :, :, at, :, lanes(c)],
                      DQ + side, DQ + 1 - side, c, (sec, ha, peer[side]))

    def ext_part(side, c):
        return remote(pz_send.at[:, :, :, :, lanes(c)], pz_recv.at[:, :, :, :, lanes(c)],
                      EXT_PART, EXT_PART, c, (sec, ha, peer[side]))

    def y_part(c):
        return remote(py_send.at[:, :, :, :, lanes(c)], py_recv.at[:, :, :, :, lanes(c)],
                      Y_PART, Y_PART, c, (sec, other, wa))

    def out_q(c):
        return remote(dq.at[:, :, :, :, lanes(c)], out.at[0, :, :, :, :, lanes(c)],
                      OUT_Q, OUT_Q, c, (before, ha, wa))

    def out_kv(c):
        return remote(dkv.at[:, :, :, :, :, lanes(c)], out.at[pl.ds(1, 2), :, :, :, :, lanes(c)],
                      OUT_KV, OUT_KV, c, (before, ha, wa))

    def if_(cond, action):
        pl.when(cond)(action)

    def leaving(c, action):
        moved = keys_move(c)
        for side in (0, 1):
            if_(has[side] & rim & jnp.logical_not(moved), lambda: action(side, True))
            if_(has[side] & jnp.logical_not(rim), lambda: action(side, False))

    def coming(c, action):
        moved = keys_move(c)
        for side in (0, 1):
            if_(by_rim[side] & jnp.logical_not(moved), lambda: action(side, True))
            if_(has[side] & jnp.logical_not(by_rim[side]), lambda: action(side, False))

    def exchanged(c, action):
        moved = keys_move(c)
        for side in (0, 1):
            wide = (rim | by_rim[side]) & jnp.logical_not(moved)
            if_(has[side] & wide, lambda: action(side, True))
            if_(has[side] & jnp.logical_not(wide), lambda: action(side, False))

    def keys_leave(c, action):
        for side in (0, 1):
            if_(by_rim[side] & keys_move(c), lambda: action(side))

    def keys_come(c, action):
        for side in (0, 1):
            if_(has[side] & rim & keys_move(c), lambda: action(side))

    def stage_send(c):
        y_kv(c).start()
        leaving(c, lambda side, both: z_q(side, c, both).start())
        keys_leave(c, lambda side: ext(side, c).start())

    def passes_corner(c):
        return (by_rim[0] | by_rim[1]) & keys_move(c)

    def stage_corner(c):
        if_(passes_corner(c), lambda: y_kv(c).wait_recv())
        keys_leave(c, lambda side: corner(side, c).start())

    def block(ref, lead, col, ch, n):
        return ref[lead + (slice(None), slice(None), col, slice(None), ch)].reshape(n, HEAD_DIM)

    def joined(ref, lead, at, ch, n):
        return jnp.concatenate([block(ref, lead, col, ch, n) for col in at])

    def first_phase(k, v, qh, gh, bias_of, e_ref, dp_ref, st_ref):
        s = dot(k, qh, ((1,), (1,))) * scale
        s = (s.reshape(-1, per_key, s.shape[1]) + bias_of).reshape(s.shape)
        top = jnp.max(s, axis=0, keepdims=True)
        e = jnp.exp(s - top)
        dp = dot(v, gh, ((1,), (1,)))
        total = jnp.sum(e, axis=0, keepdims=True)
        lse = top + jnp.log(total)
        mean = jnp.sum(e * dp, axis=0, keepdims=True) / total
        e_ref[...] = e
        dp_ref[...] = dp
        st_ref[0:1] = top
        st_ref[1:2] = lse
        st_ref[2:3] = mean
        return lse, mean

    def second_phase(k, qh, gh, e_ref, dp_ref, st_ref, lse_other, mean_other):
        factor, delta = merge(st_ref[0:1], st_ref[1:2], st_ref[2:3], lse_other, mean_other)
        p = e_ref[...] * factor
        ds = (p * (dp_ref[...] - delta)).astype(BF16)
        return (dot(ds, qh, ((1,), (0,))) * scale, dot(p.astype(BF16), gh, ((1,), (0,))),
                dot(ds, k, ((0,), (0,))) * scale)

    def own_first(key_cols, c, j):
        ch, b = channels(c, j), lax.rem(c, slots // HEADS_PER_CHUNK) * HEADS_PER_CHUNK + j
        n = key_cols * per_key
        lse, mean = first_phase(
            joined(kx, (0,), range(key_cols), ch, per_key), joined(kx, (1,), range(key_cols), ch, per_key),
            joined(q, (), range(cols), ch, per_col), joined(go, (), range(cols), ch, per_col),
            bias[...], e_own.at[b, 0:n], dp_own.at[b, 0:n], st_own.at[b])
        for row, value in ((4 * j, lse), (4 * j + 1, mean)):
            for side, order in ((0, (0, 1)), (1, (1, 0))):
                for n, col in enumerate(order):
                    stat_send[side, c, row:row + 1, n * per_col:(n + 1) * per_col] = (
                        value[:, col * per_col:(col + 1) * per_col])

    def own_second(key_cols, c, j):
        ch, b = channels(c, j), lax.rem(c, slots // HEADS_PER_CHUNK) * HEADS_PER_CHUNK + j
        n = key_cols * per_key
        if key_cols > cols:
            lse_other, mean_other = LOW, 0.0
        else:
            def pick(row):
                low = jnp.where(has[0], stat_recv[0, c, row:row + 1, 0:per_col],
                                stat_recv[1, c, row:row + 1, per_col:2 * per_col])
                high = jnp.where(has[1], stat_recv[1, c, row:row + 1, 0:per_col],
                                 stat_recv[0, c, row:row + 1, per_col:2 * per_col])
                return jnp.concatenate([low, high], axis=1)

            lse_other, mean_other = pick(4 * j + 2), pick(4 * j + 3)
        dk, dv, dqh = second_phase(
            joined(kx, (0,), range(key_cols), ch, per_key),
            joined(q, (), range(cols), ch, per_col), joined(go, (), range(cols), ch, per_col),
            e_own.at[b, 0:n], dp_own.at[b, 0:n], st_own.at[b], lse_other, mean_other)
        for i, grad in enumerate((dk, dv)):
            for col in range(key_cols):
                part = grad[col * per_key:(col + 1) * per_key].reshape(grid_t, rows + 1, tok, HEAD_DIM)
                if col < cols:
                    acc[i, :, :, col, :, ch] = part
                else:
                    pz_send[i, :, :, :, ch] = part.astype(BF16)
        for col in range(cols):
            dqa[:, :, col, :, ch] = dqh[col * per_col:(col + 1) * per_col].reshape(grid_t, rows, tok, HEAD_DIM)

    def columns(side, both):
        return (near[1 - side], near[side]) if both else (near[1 - side],)

    def z_first(side, both, c, j):
        ch, b = channels(c, j), lax.rem(c, slots // HEADS_PER_CHUNK) * HEADS_PER_CHUNK + j
        at = columns(side, both)
        n = len(at) * per_col
        lse, mean = first_phase(
            block(kx, (0,), near[side], ch, per_key), block(kx, (1,), near[side], ch, per_key),
            joined(qz, (side, 0), at, ch, per_col), joined(qz, (side, 1), at, ch, per_col),
            bias_z[side, :, 0:n], e_z.at[side, b, :, 0:n], dp_z.at[side, b, :, 0:n], st_z.at[side, b, :, 0:n])
        stat_send[side, c, 4 * j + 2:4 * j + 3, 0:n] = lse
        stat_send[side, c, 4 * j + 3:4 * j + 4, 0:n] = mean

    def z_second(side, both, c, j):
        ch, b = channels(c, j), lax.rem(c, slots // HEADS_PER_CHUNK) * HEADS_PER_CHUNK + j
        at = columns(side, both)
        n = len(at) * per_col
        dk, dv, dqh = second_phase(
            block(kx, (0,), near[side], ch, per_key),
            joined(qz, (side, 0), at, ch, per_col), joined(qz, (side, 1), at, ch, per_col),
            e_z.at[side, b, :, 0:n], dp_z.at[side, b, :, 0:n], st_z.at[side, b, :, 0:n],
            stat_recv[side, c, 4 * j:4 * j + 1, 0:n], stat_recv[side, c, 4 * j + 1:4 * j + 2, 0:n])
        for i, grad in enumerate((dk, dv)):
            acc[i, :, :, near[side], :, ch] += grad.reshape(grid_t, rows + 1, tok, HEAD_DIM)
        for m, col in enumerate(at):
            part = dqh[m * per_col:(m + 1) * per_col].astype(BF16)
            dqz_send[side, :, :, col, :, ch] = part.reshape(grid_t, rows, tok, HEAD_DIM)

    def heads(action):
        for j in range(HEADS_PER_CHUNK):
            action(j)

    def stage_first(c):
        if_(jnp.logical_not(passes_corner(c)), lambda: y_kv(c).wait_recv())

        def arrive(side):
            ext(1 - side, c).wait_recv()
            corner(1 - side, c).wait_recv()

        keys_come(c, arrive)
        far = rim & keys_move(c)
        if_(far, lambda: heads(lambda j: own_first(cols + 1, c, j)))
        if_(jnp.logical_not(far), lambda: heads(lambda j: own_first(cols, c, j)))

        def from_side(side, both):
            z_q(1 - side, c, both).wait_recv()
            heads(lambda j: z_first(side, both, c, j))

        coming(c, from_side)
        exchanged(c, lambda side, both: stat(side, c, both).start())

    def send_y(c):
        py_send[:, :, :, :, lanes(c)] = acc[:, :, rows, :, :, lanes(c)].astype(BF16)
        y_part(c).start()

    def stage_second(c):
        exchanged(c, lambda side, both: stat(1 - side, c, both).wait_recv())
        far = rim & keys_move(c)
        if_(far, lambda: heads(lambda j: own_second(cols + 1, c, j)))
        if_(jnp.logical_not(far), lambda: heads(lambda j: own_second(cols, c, j)))
        keys_come(c, lambda side: ext_part(side, c).start())

        def from_side(side, both):
            heads(lambda j: z_second(side, both, c, j))
            dq_back(side, c, both).start()

        coming(c, from_side)
        if_(jnp.logical_not(passes_corner(c)), lambda: send_y(c))

    def stage_fold(c):
        ch = lanes(c)

        def back(side, both):
            dq_back(1 - side, c, both).wait_recv()
            for col in (range(cols) if both else (near[side],)):
                dqa[:, :, col, :, ch] += dqz_recv[side, :, :, col, :, ch].astype(F32)

        leaving(c, back)
        dq[:, :, :, :, ch] = dqa[:, :, :, :, ch].astype(BF16)
        out_q(c).start()

        def fold(side):
            ext_part(1 - side, c).wait_recv()
            for i in (0, 1):
                acc[i, :, :, near[side], :, ch] += pz_recv[i, :, :, :, ch].astype(F32)

        keys_leave(c, fold)
        if_(passes_corner(c), lambda: send_y(c))

    def stage_out(c):
        ch = lanes(c)
        y_part(c).wait_recv()
        acc[:, :, edge, :, :, ch] += py_recv[:, :, :, :, ch].astype(F32)
        dkv[:, :, :, :, :, ch] = acc[:, :, 0:rows, :, :, ch].astype(BF16)
        out_kv(c).start()

    for c in range(AHEAD):
        stage_send(c)
    for load in loads:
        load.start()

    n_q = cols * per_col
    lane = lax.broadcasted_iota(jnp.int32, (1, n_q), 1)
    first = jnp.zeros((1, n_q), F32)
    for c in range(cols):
        for t in range(grid_t):
            for r in range(rows):
                tile = (c * grid_t + t) * rows + r
                first = jnp.where(lane // tok == tile, starts[r, c, t].astype(F32), first)
    first_send[...] = jnp.broadcast_to(first, first_send.shape)

    def first_copy(side):
        return pltpu.make_async_remote_copy(
            src_ref=first_send, dst_ref=first_recv.at[1 - side], send_sem=first_sem.at[0, side],
            recv_sem=first_sem.at[1, 1 - side], device_id=(sec, ha, peer[side]), device_id_type=MESH)

    for side in (0, 1):
        if_(has[side], lambda: first_copy(side).start())

    def window(ref, begin):
        per_t = (rows + 1) * tok
        for t in range(grid_t):
            seen = (begin <= t) & (begin + 2 >= t)
            row = jnp.where(seen, 0.0, LOW).astype(F32)
            ref[t * per_t:(t + 1) * per_t, :] = jnp.broadcast_to(row, (per_t, n_q))

    window(bias, first)
    for c in range(CORNERS_AHEAD):
        stage_corner(c)
    for side in (0, 1):
        def _(side=side):
            first_copy(1 - side).wait_recv()
            begin = jnp.concatenate(
                [first_recv[side, 0:1, col * per_col:(col + 1) * per_col] for col in columns(side, True)], axis=1)
            window(bias_z.at[side], begin)
        if_(has[side], _)
    for load in loads:
        load.wait()

    def step(i, carry):
        if_(i + AHEAD < chunks, lambda: stage_send(i + AHEAD))
        if_(i + CORNERS_AHEAD < chunks, lambda: stage_corner(i + CORNERS_AHEAD))
        if_(i < chunks, lambda: stage_first(i))
        if_((i >= STAT_LAG) & (i < chunks + STAT_LAG), lambda: stage_second(i - STAT_LAG))
        if_((i >= FOLD_LAG) & (i < chunks + FOLD_LAG), lambda: stage_fold(i - FOLD_LAG))
        if_(i >= OUT_LAG, lambda: stage_out(i - OUT_LAG))
        return carry

    lax.fori_loop(0, chunks + OUT_LAG, step, 0)

    for side in (0, 1):
        if_(has[side], lambda: first_copy(side).wait_send())

    def finish(c, carry):
        y_kv(c).wait_send()
        y_part(c).wait_send()
        leaving(c, lambda side, both: z_q(side, c, both).wait_send())

        def keys_sent(side):
            ext(side, c).wait_send()
            corner(side, c).wait_send()

        keys_leave(c, keys_sent)
        keys_come(c, lambda side: ext_part(side, c).wait_send())
        exchanged(c, lambda side, both: stat(side, c, both).wait_send())
        coming(c, lambda side, both: dq_back(side, c, both).wait_send())
        out_q(c).wait()
        out_kv(c).wait()
        return carry

    lax.fori_loop(0, chunks, finish, 0)


def copy_kernel(src, dst, held, sems):
    parts = [(i, t) for i in range(src.shape[0]) for t in range(src.shape[1])]
    come = [pltpu.make_async_copy(src.at[p], held.at[p], sems.at[0, n]) for n, p in enumerate(parts)]
    go = [pltpu.make_async_copy(held.at[p], dst.at[p], sems.at[1, n]) for n, p in enumerate(parts)]
    for copy in come:
        copy.start()
    for a, b in zip(come, go):
        a.wait()
        b.start()
    for copy in go:
        copy.wait()


def local(mesh_sizes, queries, keys_values, grad_out, time_start):
    n_sec, n_ha, n_wa = mesh_sizes
    q, kv, go = queries[0], keys_values[:, 0], grad_out[0]
    grid_t, rows, cols, tok, channels = q.shape
    assert n_ha == 2 and rows == 2 and cols == 2 and n_wa >= 4 and n_sec >= 2
    width = HEADS_PER_CHUNK * HEAD_DIM
    assert channels % width == 0 and 4 * HEADS_PER_CHUNK <= 8
    chunks = channels // width
    assert chunks >= AHEAD >= CORNERS_AHEAD
    per_col, per_key = grid_t * rows * tok, grid_t * (rows + 1) * tok
    n_q = cols * per_col
    slots = (STAT_LAG + 1) * HEADS_PER_CHUNK
    stay = pl.BlockSpec(memory_space=pl.ANY)
    vmem = pltpu.VMEM
    out = pl.pallas_call(
        functools.partial(kernel, (n_sec, n_ha, n_wa, chunks, width)),
        out_shape=jax.ShapeDtypeStruct((3,) + q.shape, BF16),
        in_specs=[pl.BlockSpec(memory_space=pltpu.SMEM), stay, stay, stay],
        out_specs=pl.BlockSpec(memory_space=pl.ANY),
        scratch_shapes=[
            vmem(q.shape, BF16),
            vmem(go.shape, BF16),
            vmem((2, grid_t, rows + 1, cols + 1, tok, channels), BF16),
            vmem((2, 2) + q.shape, BF16),
            pltpu.SemaphoreType.DMA((3,)),
            vmem((8, n_q), F32),
            vmem((2, 8, n_q), F32),
            pltpu.SemaphoreType.DMA((2, 2)),
            vmem((per_key, n_q), F32),
            vmem((2, per_key, n_q), F32),
            vmem((slots, (cols + 1) * per_key, n_q), F32),
            vmem((slots, (cols + 1) * per_key, n_q), F32),
            vmem((slots, 8, n_q), F32),
            vmem((2, slots, per_key, n_q), F32),
            vmem((2, slots, per_key, n_q), F32),
            vmem((2, slots, 8, n_q), F32),
            vmem((2, chunks, 8, n_q), F32),
            vmem((2, chunks, 8, n_q), F32),
            vmem((2, grid_t, rows + 1, cols, tok, channels), F32),
            vmem(q.shape, F32),
            vmem((2,) + q.shape, BF16),
            vmem((2,) + q.shape, BF16),
            vmem((2, grid_t, rows + 1, tok, channels), BF16),
            vmem((2, grid_t, rows + 1, tok, channels), BF16),
            vmem((2, grid_t, cols, tok, channels), BF16),
            vmem((2, grid_t, cols, tok, channels), BF16),
            vmem(q.shape, BF16),
            vmem((2,) + q.shape, BF16),
            pltpu.SemaphoreType.DMA((KINDS, chunks)),
            pltpu.SemaphoreType.DMA((KINDS, chunks)),
        ],
        compiler_params=pltpu.CompilerParams(
            collective_id=0, has_side_effects=True, vmem_limit_bytes=60 * 1024 * 1024
        ),
    )(time_start.transpose(1, 2, 0), q, kv, go)
    out = pl.pallas_call(
        copy_kernel,
        out_shape=jax.ShapeDtypeStruct(out.shape, BF16),
        in_specs=[pl.BlockSpec(memory_space=pl.ANY)],
        out_specs=pl.BlockSpec(memory_space=pl.ANY),
        scratch_shapes=[pltpu.VMEM(out.shape, BF16), pltpu.SemaphoreType.DMA((2, 3 * grid_t))],
    )(out)
    return out[:, None]


def solution(mesh):
    sizes = (mesh.shape["section"], mesh.shape["ha"], mesh.shape["wa"])
    return jax.shard_map(
        functools.partial(local, sizes),
        mesh=mesh,
        in_specs=(
            P("section", None, "ha", "wa", None, None),
            P(None, "section", None, "ha", "wa", None, None),
            P("section", None, "ha", "wa", None, None),
            P(None, "ha", "wa"),
        ),
        out_specs=P(None, "section", None, "ha", "wa", None, None),
        check_vma=False,
    )
```

```python
import functools

import jax
import jax.numpy as jnp
from jax import lax
from jax.experimental import pallas as pl
from jax.experimental.pallas import tpu as pltpu
from jax.sharding import PartitionSpec as P

HEAD_DIM = 128
HEADS_PER_CHUNK = 1
MESH = pl.DeviceIdType.MESH
F32 = jnp.float32
BF16 = jnp.bfloat16

Y_KV, Z_Q, Z_GO, EXT, CORNER, STAT, DQ, EXT_PART, Y_PART, OUT_Q, OUT_KV, KINDS = 0, 1, 3, 5, 6, 7, 9, 11, 12, 13, 14, 15

AHEAD = 3
CORNERS_AHEAD = 2
STAT_LAG = 2
FOLD_LAG = 4
OUT_LAG = 6
LOW = -1e30
VMEM_KIB = 56000


def dot(a, b, contract):
    return lax.dot_general(a, b, ((contract[0], contract[1]), ((), ())), preferred_element_type=F32)


def merge(top, lse, mean, lse_other, mean_other):
    most = jnp.maximum(lse, lse_other)
    w, w_other = jnp.exp(lse - most), jnp.exp(lse_other - most)
    inv = 1.0 / (w + w_other)
    return jnp.exp(top - most) * inv, (w * mean + w_other * mean_other) * inv


def kernel(sizes, starts, q_in, kv_in, go_in, out, q, go, kx, qz, load_sem, first_send, first_recv, first_sem, bias,
           bias_z, e_own, dp_own, st_own, e_z, dp_z, st_z, stat_send, stat_recv, acc, dqa, dqz_send, dqz_recv,
           pz_send, pz_recv, py_send, py_recv, dq, dkv, send_sem, recv_sem):
    n_sec, n_ha, n_wa, chunks, width = sizes
    grid_t, rows, cols, tok, _ = q.shape
    per_col = grid_t * rows * tok
    per_key = grid_t * (rows + 1) * tok
    slots = e_own.shape[0]
    sec, ha, wa = lax.axis_index("section"), lax.axis_index("ha"), lax.axis_index("wa")
    before = lax.rem(sec + n_sec - 1, n_sec)
    after = lax.rem(sec + 1, n_sec)
    other = 1 - ha
    edge = other * (rows - 1)
    has = (wa > 0, wa < n_wa - 1)
    peer = (wa - 1, wa + 1)
    near = (0, cols - 1)
    rim = (wa == 0) | (wa == n_wa - 1)
    by_rim = (wa == 1, wa == n_wa - 2)
    scale = HEAD_DIM ** (-0.5)

    loads = [pltpu.make_async_copy(src, dst, load_sem.at[n]) for n, (src, dst) in enumerate(
        ((q_in, q), (kv_in, kx.at[:, :, 0:rows, 0:cols]), (go_in, go)))]
    n_q = cols * per_col
    lane = lax.broadcasted_iota(jnp.int32, (1, n_q), 1)
    first = jnp.zeros((1, n_q), F32)
    for c in range(cols):
        for t in range(grid_t):
            for r in range(rows):
                tile = (c * grid_t + t) * rows + r
                first = jnp.where(lane // tok == tile, starts[r, c, t].astype(F32), first)
    first_send[...] = jnp.broadcast_to(first, first_send.shape)

    barrier = pltpu.get_barrier_semaphore()
    pl.semaphore_signal(barrier, inc=1, device_id=(before, ha, wa), device_id_type=MESH)
    pl.semaphore_signal(barrier, inc=1, device_id=(after, ha, wa), device_id_type=MESH)
    pl.semaphore_signal(barrier, inc=1, device_id=(sec, other, wa), device_id_type=MESH)
    for side in (0, 1):
        @pl.when(has[side])
        def _():
            pl.semaphore_signal(barrier, inc=1, device_id=(sec, ha, peer[side]), device_id_type=MESH)
    pl.semaphore_wait(barrier, 3 + jnp.minimum(wa, 1) + jnp.minimum(n_wa - 1 - wa, 1))

    def keys_move(c):
        return (lax.rem(c, 2) == 1) & (c < chunks - 2)

    def lanes(c):
        return pl.ds(pl.multiple_of(c * width, width), width)

    def channels(c, j):
        return pl.ds(pl.multiple_of(c * width + j * HEAD_DIM, HEAD_DIM), HEAD_DIM)

    def remote(src, dst, sent, arrived, c, device):
        return pltpu.make_async_remote_copy(
            src_ref=src, dst_ref=dst, send_sem=send_sem.at[sent, c], recv_sem=recv_sem.at[arrived, c],
            device_id=device, device_id_type=MESH)

    def y_kv(c):
        return remote(kv_in.at[:, :, edge, :, :, lanes(c)], kx.at[:, :, rows, 0:cols, :, lanes(c)],
                      Y_KV, Y_KV, c, (sec, other, wa))

    class Pair:
        def __init__(self, *copies):
            self.copies = copies

        def start(self):
            for copy in self.copies:
                copy.start()

        def wait_send(self):
            for copy in self.copies:
                copy.wait_send()

        def wait_recv(self):
            for copy in self.copies:
                copy.wait_recv()

    def z_q(side, c, both):
        col = near[side]
        at = slice(0, cols) if both else slice(col, col + 1)
        return Pair(*(
            remote(src.at[:, :, at, :, lanes(c)], qz.at[1 - side, n, :, :, at, :, lanes(c)],
                   kind + side, kind + 1 - side, c, (sec, ha, peer[side]))
            for n, (src, kind) in enumerate(((q_in, Z_Q), (go_in, Z_GO)))))

    def ext(side, c):
        return remote(kv_in.at[:, :, :, near[side], :, lanes(c)], kx.at[:, :, 0:rows, cols, :, lanes(c)],
                      EXT, EXT, c, (sec, ha, peer[side]))

    def corner(side, c):
        return remote(kx.at[:, :, rows, near[side], :, lanes(c)], kx.at[:, :, rows, cols, :, lanes(c)],
                      CORNER, CORNER, c, (sec, ha, peer[side]))

    def stat(side, c, both):
        at = slice(0, cols if both else 1)
        return remote(stat_send.at[side, c, :, at], stat_recv.at[1 - side, c, :, at],
                      STAT + side, STAT + 1 - side, c, (sec, ha, peer[side]))

    def dq_back(side, c, both):
        col = near[1 - side]
        at = slice(0, cols) if both else slice(col, col + 1)
        return remote(dqz_send.at[side, :, :, at, :, lanes(c)], dqz_recv.at[1 - side, :, :, at, :, lanes(c)],
                      DQ + side, DQ + 1 - side, c, (sec, ha, peer[side]))

    def ext_part(side, c):
        return remote(pz_send.at[:, :, :, :, lanes(c)], pz_recv.at[:, :, :, :, lanes(c)],
                      EXT_PART, EXT_PART, c, (sec, ha, peer[side]))

    def y_part(c):
        return remote(py_send.at[:, :, :, :, lanes(c)], py_recv.at[:, :, :, :, lanes(c)],
                      Y_PART, Y_PART, c, (sec, other, wa))

    def out_q(at):
        return remote(dq.at[:, :, :, :, at], out.at[0, :, :, :, :, at], OUT_Q, OUT_Q, 0, (before, ha, wa))

    def out_kv(at):
        return remote(dkv.at[:, :, :, :, :, at], out.at[pl.ds(1, 2), :, :, :, :, at],
                      OUT_KV, OUT_KV, 0, (before, ha, wa))

    def if_(cond, action):
        pl.when(cond)(action)

    def leaving(c, action):
        moved = keys_move(c)
        for side in (0, 1):
            if_(has[side] & rim & jnp.logical_not(moved), lambda: action(side, True))
            if_(has[side] & jnp.logical_not(rim), lambda: action(side, False))

    def coming(c, action):
        moved = keys_move(c)
        for side in (0, 1):
            if_(by_rim[side] & jnp.logical_not(moved), lambda: action(side, True))
            if_(has[side] & jnp.logical_not(by_rim[side]), lambda: action(side, False))

    def exchanged(c, action):
        moved = keys_move(c)
        for side in (0, 1):
            wide = (rim | by_rim[side]) & jnp.logical_not(moved)
            if_(has[side] & wide, lambda: action(side, True))
            if_(has[side] & jnp.logical_not(wide), lambda: action(side, False))

    def keys_leave(c, action):
        for side in (0, 1):
            if_(by_rim[side] & keys_move(c), lambda: action(side))

    def keys_come(c, action):
        for side in (0, 1):
            if_(has[side] & rim & keys_move(c), lambda: action(side))

    def stage_send(c):
        y_kv(c).start()
        leaving(c, lambda side, both: z_q(side, c, both).start())
        keys_leave(c, lambda side: ext(side, c).start())

    def passes_corner(c):
        return (by_rim[0] | by_rim[1]) & keys_move(c)

    def stage_corner(c):
        if_(passes_corner(c), lambda: y_kv(c).wait_recv())
        keys_leave(c, lambda side: corner(side, c).start())

    def block(ref, lead, col, ch, n):
        return ref[lead + (slice(None), slice(None), col, slice(None), ch)].reshape(n, HEAD_DIM)

    def joined(ref, lead, at, ch, n):
        return jnp.concatenate([block(ref, lead, col, ch, n) for col in at])

    def first_phase(k, v, qh, gh, bias_of, e_ref, dp_ref, st_ref):
        s = dot(k, qh, ((1,), (1,))) * scale
        s = (s.reshape(-1, per_key, s.shape[1]) + bias_of).reshape(s.shape)
        top = jnp.max(s, axis=0, keepdims=True)
        e = jnp.exp(s - top)
        dp = dot(v, gh, ((1,), (1,)))
        total = jnp.sum(e, axis=0, keepdims=True)
        lse = top + jnp.log(total)
        mean = jnp.sum(e * dp, axis=0, keepdims=True) / total
        e_ref[...] = e
        dp_ref[...] = dp
        st_ref[0:1] = top
        st_ref[1:2] = lse
        st_ref[2:3] = mean
        return lse, mean

    def second_phase(k, qh, gh, e_ref, dp_ref, st_ref, lse_other, mean_other):
        factor, delta = merge(st_ref[0:1], st_ref[1:2], st_ref[2:3], lse_other, mean_other)
        p = e_ref[...] * factor
        ds = (p * (dp_ref[...] - delta)).astype(BF16)
        return (dot(ds, qh, ((1,), (0,))) * scale, dot(p.astype(BF16), gh, ((1,), (0,))),
                dot(ds, k, ((0,), (0,))) * scale)

    def own_first(key_cols, c, j):
        ch, b = channels(c, j), lax.rem(c, slots // HEADS_PER_CHUNK) * HEADS_PER_CHUNK + j
        n = key_cols * per_key
        lse, mean = first_phase(
            joined(kx, (0,), range(key_cols), ch, per_key), joined(kx, (1,), range(key_cols), ch, per_key),
            joined(q, (), range(cols), ch, per_col), joined(go, (), range(cols), ch, per_col),
            bias[...], e_own.at[b, 0:n], dp_own.at[b, 0:n], st_own.at[b])
        for row, value in enumerate((lse, mean)):
            for side, order in ((0, (0, 1)), (1, (1, 0))):
                for n, col in enumerate(order):
                    stat_send[side, c, j, n, row:row + 1] = value[:, col * per_col:(col + 1) * per_col]

    def own_second(key_cols, c, j):
        ch, b = channels(c, j), lax.rem(c, slots // HEADS_PER_CHUNK) * HEADS_PER_CHUNK + j
        n = key_cols * per_key
        if key_cols > cols:
            lse_other, mean_other = LOW, 0.0
        else:
            def pick(row):
                at = slice(row, row + 1)
                low = jnp.where(has[0], stat_recv[0, c, j, 0, at], stat_recv[1, c, j, 1, at])
                high = jnp.where(has[1], stat_recv[1, c, j, 0, at], stat_recv[0, c, j, 1, at])
                return jnp.concatenate([low, high], axis=1)

            lse_other, mean_other = pick(2), pick(3)
        dk, dv, dqh = second_phase(
            joined(kx, (0,), range(key_cols), ch, per_key),
            joined(q, (), range(cols), ch, per_col), joined(go, (), range(cols), ch, per_col),
            e_own.at[b, 0:n], dp_own.at[b, 0:n], st_own.at[b], lse_other, mean_other)
        for i, grad in enumerate((dk, dv)):
            for col in range(key_cols):
                part = grad[col * per_key:(col + 1) * per_key].reshape(grid_t, rows + 1, tok, HEAD_DIM)
                if col < cols:
                    acc[i, :, :, col, :, ch] = part
                else:
                    pz_send[i, :, :, :, ch] = part.astype(BF16)
        for col in range(cols):
            dqa[:, :, col, :, ch] = dqh[col * per_col:(col + 1) * per_col].reshape(grid_t, rows, tok, HEAD_DIM)

    def columns(side, both):
        return (near[1 - side], near[side]) if both else (near[1 - side],)

    def z_first(side, both, c, j):
        ch, b = channels(c, j), lax.rem(c, slots // HEADS_PER_CHUNK) * HEADS_PER_CHUNK + j
        at = columns(side, both)
        n = len(at) * per_col
        lse, mean = first_phase(
            block(kx, (0,), near[side], ch, per_key), block(kx, (1,), near[side], ch, per_key),
            joined(qz, (side, 0), at, ch, per_col), joined(qz, (side, 1), at, ch, per_col),
            bias_z[side, :, 0:n], e_z.at[side, b, :, 0:n], dp_z.at[side, b, :, 0:n], st_z.at[side, b, :, 0:n])
        for row, value in ((2, lse), (3, mean)):
            for m in range(len(at)):
                stat_send[side, c, j, m, row:row + 1] = value[:, m * per_col:(m + 1) * per_col]

    def z_second(side, both, c, j):
        ch, b = channels(c, j), lax.rem(c, slots // HEADS_PER_CHUNK) * HEADS_PER_CHUNK + j
        at = columns(side, both)
        n = len(at) * per_col
        dk, dv, dqh = second_phase(
            block(kx, (0,), near[side], ch, per_key),
            joined(qz, (side, 0), at, ch, per_col), joined(qz, (side, 1), at, ch, per_col),
            e_z.at[side, b, :, 0:n], dp_z.at[side, b, :, 0:n], st_z.at[side, b, :, 0:n],
            *(jnp.concatenate([stat_recv[side, c, j, m, row:row + 1] for m in range(len(at))], axis=1)
              for row in (0, 1)))
        for i, grad in enumerate((dk, dv)):
            acc[i, :, :, near[side], :, ch] += grad.reshape(grid_t, rows + 1, tok, HEAD_DIM)
        for m, col in enumerate(at):
            part = dqh[m * per_col:(m + 1) * per_col].astype(BF16)
            dqz_send[side, :, :, col, :, ch] = part.reshape(grid_t, rows, tok, HEAD_DIM)

    def heads(action):
        for j in range(HEADS_PER_CHUNK):
            action(j)

    def stage_first(c):
        if_(jnp.logical_not(passes_corner(c)), lambda: y_kv(c).wait_recv())

        def arrive(side):
            ext(1 - side, c).wait_recv()
            corner(1 - side, c).wait_recv()

        keys_come(c, arrive)
        far = rim & keys_move(c)
        if_(far, lambda: heads(lambda j: own_first(cols + 1, c, j)))
        if_(jnp.logical_not(far), lambda: heads(lambda j: own_first(cols, c, j)))

        def from_side(side, both):
            z_q(1 - side, c, both).wait_recv()
            heads(lambda j: z_first(side, both, c, j))

        coming(c, from_side)
        exchanged(c, lambda side, both: stat(side, c, both).start())

    def send_y(c):
        py_send[:, :, :, :, lanes(c)] = acc[:, :, rows, :, :, lanes(c)].astype(BF16)
        y_part(c).start()

    def stage_second(c):
        exchanged(c, lambda side, both: stat(1 - side, c, both).wait_recv())
        far = rim & keys_move(c)
        if_(far, lambda: heads(lambda j: own_second(cols + 1, c, j)))
        if_(jnp.logical_not(far), lambda: heads(lambda j: own_second(cols, c, j)))
        keys_come(c, lambda side: ext_part(side, c).start())

        def from_side(side, both):
            heads(lambda j: z_second(side, both, c, j))
            dq_back(side, c, both).start()

        coming(c, from_side)
        if_(jnp.logical_not(passes_corner(c)), lambda: send_y(c))

    def stage_fold(c):
        ch = lanes(c)

        def back(side, both):
            dq_back(1 - side, c, both).wait_recv()
            for col in (range(cols) if both else (near[side],)):
                dqa[:, :, col, :, ch] += dqz_recv[side, :, :, col, :, ch].astype(F32)

        leaving(c, back)
        dq[:, :, :, :, ch] = dqa[:, :, :, :, ch].astype(BF16)
        out_q(ch).start()

        def fold(side):
            ext_part(1 - side, c).wait_recv()
            for i in (0, 1):
                acc[i, :, :, near[side], :, ch] += pz_recv[i, :, :, :, ch].astype(F32)

        keys_leave(c, fold)
        if_(passes_corner(c), lambda: send_y(c))

    def sent(c):
        y_kv(c).wait_send()
        y_part(c).wait_send()
        leaving(c, lambda side, both: z_q(side, c, both).wait_send())

        def keys_sent(side):
            ext(side, c).wait_send()
            corner(side, c).wait_send()

        keys_leave(c, keys_sent)
        keys_come(c, lambda side: ext_part(side, c).wait_send())
        exchanged(c, lambda side, both: stat(side, c, both).wait_send())
        coming(c, lambda side, both: dq_back(side, c, both).wait_send())

    def stage_out(c):
        ch = lanes(c)
        y_part(c).wait_recv()
        acc[:, :, edge, :, :, ch] += py_recv[:, :, :, :, ch].astype(F32)
        dkv[:, :, :, :, :, ch] = acc[:, :, 0:rows, :, :, ch].astype(BF16)
        out_kv(ch).start()
        sent(c)

    def first_copy(side):
        return pltpu.make_async_remote_copy(
            src_ref=first_send, dst_ref=first_recv.at[1 - side], send_sem=first_sem.at[0, side],
            recv_sem=first_sem.at[1, 1 - side], device_id=(sec, ha, peer[side]), device_id_type=MESH)

    for side in (0, 1):
        if_(has[side], lambda: first_copy(side).start())

    for c in range(AHEAD):
        stage_send(c)
    for load in loads:
        load.start()

    def window(ref, begin):
        per_t = (rows + 1) * tok
        for t in range(grid_t):
            seen = (begin <= t) & (begin + 2 >= t)
            row = jnp.where(seen, 0.0, LOW).astype(F32)
            ref[t * per_t:(t + 1) * per_t, :] = jnp.broadcast_to(row, (per_t, n_q))

    window(bias, first)
    for c in range(CORNERS_AHEAD):
        stage_corner(c)
    for side in (0, 1):
        def _(side=side):
            first_copy(1 - side).wait_recv()
            begin = jnp.concatenate(
                [first_recv[side, 0:1, col * per_col:(col + 1) * per_col] for col in columns(side, True)], axis=1)
            window(bias_z.at[side], begin)
        if_(has[side], _)
    for load in loads:
        load.wait()

    def step(i, carry):
        if_(i + AHEAD < chunks, lambda: stage_send(i + AHEAD))
        if_(i + CORNERS_AHEAD < chunks, lambda: stage_corner(i + CORNERS_AHEAD))
        if_(i < chunks, lambda: stage_first(i))
        if_((i >= STAT_LAG) & (i < chunks + STAT_LAG), lambda: stage_second(i - STAT_LAG))
        if_((i >= FOLD_LAG) & (i < chunks + FOLD_LAG), lambda: stage_fold(i - FOLD_LAG))
        if_(i >= OUT_LAG, lambda: stage_out(i - OUT_LAG))
        return carry

    lax.fori_loop(0, chunks + OUT_LAG, step, 0)

    for side in (0, 1):
        if_(has[side], lambda: first_copy(side).wait_send())

    out_q(slice(None)).wait()
    out_kv(slice(None)).wait()


def local(mesh_sizes, queries, keys_values, grad_out, time_start):
    n_sec, n_ha, n_wa = mesh_sizes
    q, kv, go = queries[0], keys_values[:, 0], grad_out[0]
    grid_t, rows, cols, tok, channels = q.shape
    assert n_ha == 2 and rows == 2 and cols == 2 and n_wa >= 4 and n_sec >= 2
    width = HEADS_PER_CHUNK * HEAD_DIM
    assert channels % width == 0
    chunks = channels // width
    assert chunks >= AHEAD >= CORNERS_AHEAD
    per_col, per_key = grid_t * rows * tok, grid_t * (rows + 1) * tok
    n_q = cols * per_col
    slots = (STAT_LAG + 1) * HEADS_PER_CHUNK
    stay = pl.BlockSpec(memory_space=pl.ANY)
    vmem = pltpu.VMEM
    out = pl.pallas_call(
        functools.partial(kernel, (n_sec, n_ha, n_wa, chunks, width)),
        out_shape=pltpu.VMEM((3,) + q.shape, BF16),
        in_specs=[pl.BlockSpec(memory_space=pltpu.SMEM), stay, stay, stay],
        out_specs=pl.BlockSpec(memory_space=pltpu.VMEM),
        scratch_shapes=[
            vmem(q.shape, BF16),
            vmem(go.shape, BF16),
            vmem((2, grid_t, rows + 1, cols + 1, tok, channels), BF16),
            vmem((2, 2) + q.shape, BF16),
            pltpu.SemaphoreType.DMA((3,)),
            vmem((8, n_q), F32),
            vmem((2, 8, n_q), F32),
            pltpu.SemaphoreType.DMA((2, 2)),
            vmem((per_key, n_q), F32),
            vmem((2, per_key, n_q), F32),
            vmem((slots, (cols + 1) * per_key, n_q), F32),
            vmem((slots, (cols + 1) * per_key, n_q), F32),
            vmem((slots, 8, n_q), F32),
            vmem((2, slots, per_key, n_q), F32),
            vmem((2, slots, per_key, n_q), F32),
            vmem((2, slots, 8, n_q), F32),
            vmem((2, chunks, HEADS_PER_CHUNK, cols, 4, per_col), F32),
            vmem((2, chunks, HEADS_PER_CHUNK, cols, 4, per_col), F32),
            vmem((2, grid_t, rows + 1, cols, tok, channels), F32),
            vmem(q.shape, F32),
            vmem((2,) + q.shape, BF16),
            vmem((2,) + q.shape, BF16),
            vmem((2, grid_t, rows + 1, tok, channels), BF16),
            vmem((2, grid_t, rows + 1, tok, channels), BF16),
            vmem((2, grid_t, cols, tok, channels), BF16),
            vmem((2, grid_t, cols, tok, channels), BF16),
            vmem(q.shape, BF16),
            vmem((2,) + q.shape, BF16),
            pltpu.SemaphoreType.DMA((KINDS, chunks)),
            pltpu.SemaphoreType.DMA((KINDS, chunks)),
        ],
        compiler_params=pltpu.CompilerParams(
            collective_id=0, has_side_effects=True, vmem_limit_bytes=VMEM_KIB * 1024
        ),
    )(time_start.transpose(1, 2, 0), q, kv, go)
    return out[:, None]


def solution(mesh):
    sizes = (mesh.shape["section"], mesh.shape["ha"], mesh.shape["wa"])
    return jax.shard_map(
        functools.partial(local, sizes),
        mesh=mesh,
        in_specs=(
            P("section", None, "ha", "wa", None, None),
            P(None, "section", None, "ha", "wa", None, None),
            P("section", None, "ha", "wa", None, None),
            P(None, "ha", "wa"),
        ),
        out_specs=P(None, "section", None, "ha", "wa", None, None),
        check_vma=False,
    )
```

```python
import functools

import jax
import jax.numpy as jnp
from jax import lax
from jax.experimental import pallas as pl
from jax.experimental.pallas import tpu as pltpu
from jax.sharding import PartitionSpec as P

HEAD_DIM = 128
HEADS_PER_CHUNK = 1
MESH = pl.DeviceIdType.MESH
F32 = jnp.float32
BF16 = jnp.bfloat16

Y_KV, Z_Q, EXT, CORNER, STAT, DQ, EXT_PART, CORNER_PART, Y_PART, OUT, KINDS = (
    0, 1, 3, 4, 5, 7, 9, 10, 11, 12, 13)

AHEAD_Y = 5
AHEAD_Q = 3
AHEAD_E = 3
CORNERS_AHEAD = 2
STAT_LAG = 2
FOLD_LAG = 4
LOW = -1e30
VMEM_KIB = 56000


def dot(a, b, contract):
    return lax.dot_general(a, b, ((contract[0], contract[1]), ((), ())), preferred_element_type=F32)


def merge(top, lse, mean, lse_other, mean_other):
    most = jnp.maximum(lse, lse_other)
    w, w_other = jnp.exp(lse - most), jnp.exp(lse_other - most)
    inv = 1.0 / (w + w_other)
    return jnp.exp(top - most) * inv, (w * mean + w_other * mean_other) * inv


def kernel(sizes, starts, q_in, kv_in, go_in, out, qg, kx, qz, load_sem, first_send, first_recv, first_sem, bias,
           bias_z, e_own, dp_own, st_own, e_z, dp_z, st_z, stat_send, stat_recv, acc, dqz_send, dqz_recv,
           pz_send, pz_recv, pc_recv, py_send, py_recv, own, total, send_sem, recv_sem):
    n_sec, n_ha, n_wa, chunks, width = sizes
    _, grid_t, rows, cols, tok, _ = qg.shape
    per_col = grid_t * rows * tok
    per_key = grid_t * (rows + 1) * tok
    slots = e_own.shape[0]
    sec, ha, wa = lax.axis_index("section"), lax.axis_index("ha"), lax.axis_index("wa")
    before = lax.rem(sec + n_sec - 1, n_sec)
    after = lax.rem(sec + 1, n_sec)
    other = 1 - ha
    edge = other * (rows - 1)
    has = (wa > 0, wa < n_wa - 1)
    peer = (wa - 1, wa + 1)
    near = (0, cols - 1)
    rim = (wa == 0) | (wa == n_wa - 1)
    by_rim = (wa == 1, wa == n_wa - 2)
    scale = HEAD_DIM ** (-0.5)

    loads = [pltpu.make_async_copy(src, dst, load_sem.at[n]) for n, (src, dst) in enumerate(
        ((q_in, qg.at[0]), (go_in, qg.at[1]), (kv_in, kx.at[:, :, 0:rows, 0:cols])))]
    for load in loads:
        load.start()

    n_q = cols * per_col
    lane = lax.broadcasted_iota(jnp.int32, (1, n_q), 1)
    first = jnp.zeros((1, n_q), F32)
    for c in range(cols):
        for t in range(grid_t):
            for r in range(rows):
                tile = (c * grid_t + t) * rows + r
                first = jnp.where(lane // tok == tile, starts[r, c, t].astype(F32), first)
    first_send[...] = jnp.broadcast_to(first, first_send.shape)

    barrier = pltpu.get_barrier_semaphore()

    def greet(*device):
        pl.semaphore_signal(barrier, inc=1, device_id=device, device_id_type=MESH)

    greet(before, ha, wa)
    greet(after, ha, wa)
    greet(sec, other, wa)
    for side in (0, 1):
        @pl.when(has[side])
        def _():
            greet(sec, ha, peer[side])

        @pl.when(has[side] & (rim | by_rim[side]))
        def _():
            greet(sec, other, peer[side])

    sides_here = jnp.minimum(wa, 1) + jnp.minimum(n_wa - 1 - wa, 1)
    rims_here = jnp.where(rim, 1, by_rim[0].astype(jnp.int32) + by_rim[1].astype(jnp.int32))
    pl.semaphore_wait(barrier, 3 + sides_here + rims_here)

    def keys_move(c):
        return ((lax.rem(c, 5) == 2) | (lax.rem(c, 5) == 0)) & (c > 0) & (c < chunks - 2)

    def lanes(c):
        return pl.ds(pl.multiple_of(c * width, width), width)

    def within(j):
        return slice(j * HEAD_DIM, (j + 1) * HEAD_DIM)

    def channels(c, j):
        return pl.ds(pl.multiple_of(c * width + j * HEAD_DIM, HEAD_DIM), HEAD_DIM)

    def remote(src, dst, sent, arrived, c, device):
        return pltpu.make_async_remote_copy(
            src_ref=src, dst_ref=dst, send_sem=send_sem.at[sent, c], recv_sem=recv_sem.at[arrived, c],
            device_id=device, device_id_type=MESH)

    def y_kv(c):
        return remote(kx.at[:, :, edge, 0:cols, :, lanes(c)], kx.at[:, :, rows, 0:cols, :, lanes(c)],
                      Y_KV, Y_KV, c, (sec, other, wa))

    def z_q(side, c, both):
        at = slice(0, cols) if both else slice(near[side], near[side] + 1)
        return remote(qg.at[:, :, :, at, :, lanes(c)], qz.at[1 - side, :, :, :, at, :, lanes(c)],
                      Z_Q + side, Z_Q + 1 - side, c, (sec, ha, peer[side]))

    def ext(side, c):
        return remote(kx.at[:, :, 0:rows, near[side], :, lanes(c)], kx.at[:, :, 0:rows, cols, :, lanes(c)],
                      EXT, EXT, c, (sec, ha, peer[side]))

    def corner(side, c):
        return remote(kx.at[:, :, rows, near[side], :, lanes(c)], kx.at[:, :, rows, cols, :, lanes(c)],
                      CORNER, CORNER, c, (sec, ha, peer[side]))

    def stat(side, c, both):
        at = slice(0, cols if both else 1)
        return remote(stat_send.at[side, c, :, at], stat_recv.at[1 - side, c, :, at],
                      STAT + side, STAT + 1 - side, c, (sec, ha, peer[side]))

    def dq_back(side, c, both):
        col = near[1 - side]
        at = slice(0, cols) if both else slice(col, col + 1)
        return remote(dqz_send.at[side, :, :, at, :, lanes(c)], dqz_recv.at[1 - side, :, :, at, :, lanes(c)],
                      DQ + side, DQ + 1 - side, c, (sec, ha, peer[side]))

    def ext_part(side, c):
        return remote(pz_send.at[:, :, 0:rows, :, lanes(c)], pz_recv.at[:, :, :, :, lanes(c)],
                      EXT_PART, EXT_PART, c, (sec, ha, peer[side]))

    def corner_part(side, c):
        return remote(pz_send.at[:, :, rows, :, lanes(c)], pc_recv.at[:, :, :, lanes(c)],
                      CORNER_PART, CORNER_PART, c, (sec, other, peer[side]))

    def y_part(c):
        return remote(py_send.at[:, :, :, :, lanes(c)], py_recv.at[:, :, :, :, lanes(c)],
                      Y_PART, Y_PART, c, (sec, other, wa))

    def result(at):
        return remote(own.at[:, :, :, :, :, at], out.at[:, :, :, :, :, at], OUT, OUT, 0, (before, ha, wa))

    def if_(cond, action):
        pl.when(cond)(action)

    def leaving(c, action):
        moved = keys_move(c)
        for side in (0, 1):
            if_(has[side] & rim & jnp.logical_not(moved), lambda: action(side, True))
            if_(has[side] & jnp.logical_not(rim), lambda: action(side, False))

    def coming(c, action):
        moved = keys_move(c)
        for side in (0, 1):
            if_(by_rim[side] & jnp.logical_not(moved), lambda: action(side, True))
            if_(has[side] & jnp.logical_not(by_rim[side]), lambda: action(side, False))

    def exchanged(c, action):
        moved = keys_move(c)
        for side in (0, 1):
            wide = (rim | by_rim[side]) & jnp.logical_not(moved)
            if_(has[side] & wide, lambda: action(side, True))
            if_(has[side] & jnp.logical_not(wide), lambda: action(side, False))

    def keys_leave(c, action):
        for side in (0, 1):
            if_(by_rim[side] & keys_move(c), lambda: action(side))

    def keys_come(c, action):
        for side in (0, 1):
            if_(has[side] & rim & keys_move(c), lambda: action(side))

    def stage_send(c, y, z, keys):
        if y:
            y_kv(c).start()
        if z:
            leaving(c, lambda side, both: z_q(side, c, both).start())
        if keys:
            keys_leave(c, lambda side: ext(side, c).start())

    def passes_corner(c):
        return (by_rim[0] | by_rim[1]) & keys_move(c)

    def stage_corner(c):
        if_(passes_corner(c), lambda: y_kv(c).wait_recv())
        keys_leave(c, lambda side: corner(side, c).start())

    def block(ref, lead, col, ch, n):
        return ref[lead + (slice(None), slice(None), col, slice(None), ch)].reshape(n, HEAD_DIM)

    def joined(ref, lead, at, ch, n):
        return jnp.concatenate([block(ref, lead, col, ch, n) for col in at])

    def first_phase(k, v, qh, gh, bias_of, e_ref, dp_ref, st_ref):
        s = dot(k, qh, ((1,), (1,))) * scale
        s = (s.reshape(-1, per_key, s.shape[1]) + bias_of).reshape(s.shape)
        top = jnp.max(s, axis=0, keepdims=True)
        e = jnp.exp(s - top)
        dp = dot(v, gh, ((1,), (1,)))
        total = jnp.sum(e, axis=0, keepdims=True)
        lse = top + jnp.log(total)
        mean = jnp.sum(e * dp, axis=0, keepdims=True) / total
        e_ref[...] = e
        dp_ref[...] = dp
        st_ref[0:1] = top
        st_ref[1:2] = lse
        st_ref[2:3] = mean
        return lse, mean

    def second_phase(k, qh, gh, e_ref, dp_ref, st_ref, lse_other, mean_other):
        factor, delta = merge(st_ref[0:1], st_ref[1:2], st_ref[2:3], lse_other, mean_other)
        p = e_ref[...] * factor
        ds = (p * (dp_ref[...] - delta)).astype(BF16)
        return (dot(ds, qh, ((1,), (0,))) * scale, dot(p.astype(BF16), gh, ((1,), (0,))),
                dot(ds, k, ((0,), (0,))) * scale)

    def own_first(key_cols, c, j):
        ch, b = channels(c, j), lax.rem(c, slots // HEADS_PER_CHUNK) * HEADS_PER_CHUNK + j
        n = key_cols * per_key
        lse, mean = first_phase(
            joined(kx, (0,), range(key_cols), ch, per_key), joined(kx, (1,), range(key_cols), ch, per_key),
            joined(qg, (0,), range(cols), ch, per_col), joined(qg, (1,), range(cols), ch, per_col),
            bias[...], e_own.at[b, 0:n], dp_own.at[b, 0:n], st_own.at[b])
        for row, value in enumerate((lse, mean)):
            for side, order in ((0, (0, 1)), (1, (1, 0))):
                for n, col in enumerate(order):
                    stat_send[side, c, j, n, row:row + 1] = value[:, col * per_col:(col + 1) * per_col]

    def own_second(key_cols, c, j):
        ch, b = channels(c, j), lax.rem(c, slots // HEADS_PER_CHUNK) * HEADS_PER_CHUNK + j
        n = key_cols * per_key
        if key_cols > cols:
            lse_other, mean_other = LOW, 0.0
        else:
            def pick(row):
                at = slice(row, row + 1)
                low = jnp.where(has[0], stat_recv[0, c, j, 0, at], stat_recv[1, c, j, 1, at])
                high = jnp.where(has[1], stat_recv[1, c, j, 0, at], stat_recv[0, c, j, 1, at])
                return jnp.concatenate([low, high], axis=1)

            lse_other, mean_other = pick(2), pick(3)
        dk, dv, dqh = second_phase(
            joined(kx, (0,), range(key_cols), ch, per_key),
            joined(qg, (0,), range(cols), ch, per_col), joined(qg, (1,), range(cols), ch, per_col),
            e_own.at[b, 0:n], dp_own.at[b, 0:n], st_own.at[b], lse_other, mean_other)
        for i, grad in enumerate((dk, dv)):
            for col in range(key_cols):
                part = grad[col * per_key:(col + 1) * per_key].reshape(grid_t, rows + 1, tok, HEAD_DIM)
                if col < cols:
                    acc[i, :, :, col, :, within(j)] = part
                else:
                    pz_send[i, :, :, :, ch] = part.astype(BF16)
        for col in range(cols):
            part = dqh[col * per_col:(col + 1) * per_col].astype(BF16)
            own[0, :, :, col, :, ch] = part.reshape(grid_t, rows, tok, HEAD_DIM)

    def columns(side, both):
        return (near[1 - side], near[side]) if both else (near[1 - side],)

    def z_first(side, both, c, j):
        ch, b = channels(c, j), lax.rem(c, slots // HEADS_PER_CHUNK) * HEADS_PER_CHUNK + j
        at = columns(side, both)
        n = len(at) * per_col
        lse, mean = first_phase(
            block(kx, (0,), near[side], ch, per_key), block(kx, (1,), near[side], ch, per_key),
            joined(qz, (side, 0), at, ch, per_col), joined(qz, (side, 1), at, ch, per_col),
            bias_z[side, :, 0:n], e_z.at[side, b, :, 0:n], dp_z.at[side, b, :, 0:n], st_z.at[side, b, :, 0:n])
        for row, value in ((2, lse), (3, mean)):
            for m in range(len(at)):
                stat_send[side, c, j, m, row:row + 1] = value[:, m * per_col:(m + 1) * per_col]

    def z_second(side, both, c, j):
        ch, b = channels(c, j), lax.rem(c, slots // HEADS_PER_CHUNK) * HEADS_PER_CHUNK + j
        at = columns(side, both)
        n = len(at) * per_col
        dk, dv, dqh = second_phase(
            block(kx, (0,), near[side], ch, per_key),
            joined(qz, (side, 0), at, ch, per_col), joined(qz, (side, 1), at, ch, per_col),
            e_z.at[side, b, :, 0:n], dp_z.at[side, b, :, 0:n], st_z.at[side, b, :, 0:n],
            *(jnp.concatenate([stat_recv[side, c, j, m, row:row + 1] for m in range(len(at))], axis=1)
              for row in (0, 1)))
        for i, grad in enumerate((dk, dv)):
            acc[i, :, :, near[side], :, within(j)] += grad.reshape(grid_t, rows + 1, tok, HEAD_DIM)
        for m, col in enumerate(at):
            part = dqh[m * per_col:(m + 1) * per_col].astype(BF16)
            dqz_send[side, :, :, col, :, ch] = part.reshape(grid_t, rows, tok, HEAD_DIM)

    def heads(action):
        for j in range(HEADS_PER_CHUNK):
            action(j)

    def stage_first(c):
        if_(jnp.logical_not(passes_corner(c)), lambda: y_kv(c).wait_recv())

        def arrive(side):
            ext(1 - side, c).wait_recv()
            corner(1 - side, c).wait_recv()

        keys_come(c, arrive)
        far = rim & keys_move(c)
        if_(far, lambda: heads(lambda j: own_first(cols + 1, c, j)))
        if_(jnp.logical_not(far), lambda: heads(lambda j: own_first(cols, c, j)))

        def from_side(side, both):
            z_q(1 - side, c, both).wait_recv()
            heads(lambda j: z_first(side, both, c, j))

        coming(c, from_side)
        exchanged(c, lambda side, both: stat(side, c, both).start())

    def stage_second(c):
        exchanged(c, lambda side, both: stat(1 - side, c, both).wait_recv())
        far = rim & keys_move(c)
        if_(far, lambda: heads(lambda j: own_second(cols + 1, c, j)))
        if_(jnp.logical_not(far), lambda: heads(lambda j: own_second(cols, c, j)))

        def extra(side):
            ext_part(side, c).start()
            corner_part(side, c).start()

        keys_come(c, extra)

        def from_side(side, both):
            heads(lambda j: z_second(side, both, c, j))
            dq_back(side, c, both).start()

        coming(c, from_side)
        ch = lanes(c)
        py_send[:, :, :, :, ch] = acc[:, :, rows].astype(BF16)
        y_part(c).start()
        own[1:3, :, :, :, :, ch] = acc[:, :, 0:rows].astype(BF16)

    def sent(c):
        y_kv(c).wait_send()
        leaving(c, lambda side, both: z_q(side, c, both).wait_send())

        def keys_sent(side):
            ext(side, c).wait_send()
            corner(side, c).wait_send()

        keys_leave(c, keys_sent)

        def extra_sent(side):
            ext_part(side, c).wait_send()
            corner_part(side, c).wait_send()

        keys_come(c, extra_sent)
        exchanged(c, lambda side, both: stat(side, c, both).wait_send())
        coming(c, lambda side, both: dq_back(side, c, both).wait_send())
        y_part(c).wait_send()

    def stage_fold(c):
        ch = lanes(c)
        total[...] = own[:, :, :, :, :, ch].astype(F32)

        def fold(side):
            ext_part(1 - side, c).wait_recv()
            corner_part(1 - side, c).wait_recv()
            total[1:3, :, :, near[side]] += pz_recv[:, :, :, :, ch].astype(F32)
            total[1:3, :, edge, near[side]] += pc_recv[:, :, :, ch].astype(F32)

        keys_leave(c, fold)
        y_part(c).wait_recv()
        total[1:3, :, edge] += py_recv[:, :, :, :, ch].astype(F32)

        def back(side, both):
            dq_back(1 - side, c, both).wait_recv()
            for col in (range(cols) if both else (near[side],)):
                total[0, :, :, col] += dqz_recv[side, :, :, col, :, ch].astype(F32)

        leaving(c, back)
        own[:, :, :, :, :, ch] = total[...].astype(BF16)
        result(ch).start()
        sent(c)

    def first_copy(side):
        return pltpu.make_async_remote_copy(
            src_ref=first_send, dst_ref=first_recv.at[1 - side], send_sem=first_sem.at[0, side],
            recv_sem=first_sem.at[1, 1 - side], device_id=(sec, ha, peer[side]), device_id_type=MESH)

    for side in (0, 1):
        if_(has[side], lambda: first_copy(side).start())

    for load in loads:
        load.wait()
    for c in range(max(AHEAD_Y, AHEAD_Q, AHEAD_E)):
        stage_send(c, c < AHEAD_Y, c < AHEAD_Q, c < AHEAD_E)

    def window(ref, begin):
        per_t = (rows + 1) * tok
        for t in range(grid_t):
            seen = (begin <= t) & (begin + 2 >= t)
            row = jnp.where(seen, 0.0, LOW).astype(F32)
            ref[t * per_t:(t + 1) * per_t, :] = jnp.broadcast_to(row, (per_t, n_q))

    window(bias, first)
    for c in range(CORNERS_AHEAD):
        stage_corner(c)
    for side in (0, 1):
        def _(side=side):
            first_copy(1 - side).wait_recv()
            begin = jnp.concatenate(
                [first_recv[side, 0:1, col * per_col:(col + 1) * per_col] for col in columns(side, True)], axis=1)
            window(bias_z.at[side], begin)
        if_(has[side], _)

    def step(i, carry):
        if_(i + AHEAD_Y < chunks, lambda: stage_send(i + AHEAD_Y, True, False, False))
        if_(i + AHEAD_Q < chunks, lambda: stage_send(i + AHEAD_Q, False, True, False))
        if_(i + AHEAD_E < chunks, lambda: stage_send(i + AHEAD_E, False, False, True))
        if_(i + CORNERS_AHEAD < chunks, lambda: stage_corner(i + CORNERS_AHEAD))
        if_(i < chunks, lambda: stage_first(i))
        if_((i >= STAT_LAG) & (i < chunks + STAT_LAG), lambda: stage_second(i - STAT_LAG))
        if_(i >= FOLD_LAG, lambda: stage_fold(i - FOLD_LAG))
        return carry

    lax.fori_loop(0, chunks + FOLD_LAG, step, 0)
    result(slice(None)).wait()
    for side in (0, 1):
        if_(has[side], lambda: first_copy(side).wait_send())


def local(mesh_sizes, queries, keys_values, grad_out, time_start):
    n_sec, n_ha, n_wa = mesh_sizes
    q, kv, go = queries[0], keys_values[:, 0], grad_out[0]
    grid_t, rows, cols, tok, channels = q.shape
    assert n_ha == 2 and rows == 2 and cols == 2 and n_wa >= 4 and n_sec >= 2
    width = HEADS_PER_CHUNK * HEAD_DIM
    assert channels % width == 0
    chunks = channels // width
    assert chunks >= max(AHEAD_Y, AHEAD_Q, AHEAD_E) and AHEAD_Y >= CORNERS_AHEAD
    per_col, per_key = grid_t * rows * tok, grid_t * (rows + 1) * tok
    n_q = cols * per_col
    slots = (STAT_LAG + 1) * HEADS_PER_CHUNK
    stay = pl.BlockSpec(memory_space=pl.ANY)
    vmem = pltpu.VMEM
    out = pl.pallas_call(
        functools.partial(kernel, (n_sec, n_ha, n_wa, chunks, width)),
        out_shape=pltpu.VMEM((3,) + q.shape, BF16),
        in_specs=[pl.BlockSpec(memory_space=pltpu.SMEM), stay, stay, stay],
        out_specs=pl.BlockSpec(memory_space=pltpu.VMEM),
        scratch_shapes=[
            vmem((2,) + q.shape, BF16),
            vmem((2, grid_t, rows + 1, cols + 1, tok, channels), BF16),
            vmem((2, 2) + q.shape, BF16),
            pltpu.SemaphoreType.DMA((3,)),
            vmem((8, n_q), F32),
            vmem((2, 8, n_q), F32),
            pltpu.SemaphoreType.DMA((2, 2)),
            vmem((per_key, n_q), F32),
            vmem((2, per_key, n_q), F32),
            vmem((slots, (cols + 1) * per_key, n_q), F32),
            vmem((slots, (cols + 1) * per_key, n_q), F32),
            vmem((slots, 8, n_q), F32),
            vmem((2, slots, per_key, n_q), F32),
            vmem((2, slots, per_key, n_q), F32),
            vmem((2, slots, 8, n_q), F32),
            vmem((2, chunks, HEADS_PER_CHUNK, cols, 4, per_col), F32),
            vmem((2, chunks, HEADS_PER_CHUNK, cols, 4, per_col), F32),
            vmem((2, grid_t, rows + 1, cols, tok, width), F32),
            vmem((2,) + q.shape, BF16),
            vmem((2,) + q.shape, BF16),
            vmem((2, grid_t, rows + 1, tok, channels), BF16),
            vmem((2, grid_t, rows, tok, channels), BF16),
            vmem((2, grid_t, tok, channels), BF16),
            vmem((2, grid_t, cols, tok, channels), BF16),
            vmem((2, grid_t, cols, tok, channels), BF16),
            vmem((3,) + q.shape, BF16),
            vmem((3, grid_t, rows, cols, tok, width), F32),
            pltpu.SemaphoreType.DMA((KINDS, chunks)),
            pltpu.SemaphoreType.DMA((KINDS, chunks)),
        ],
        compiler_params=pltpu.CompilerParams(
            collective_id=0, has_side_effects=True, vmem_limit_bytes=VMEM_KIB * 1024
        ),
    )(time_start.transpose(1, 2, 0), q, kv, go)
    return out[:, None]


def solution(mesh):
    sizes = (mesh.shape["section"], mesh.shape["ha"], mesh.shape["wa"])
    return jax.shard_map(
        functools.partial(local, sizes),
        mesh=mesh,
        in_specs=(
            P("section", None, "ha", "wa", None, None),
            P(None, "section", None, "ha", "wa", None, None),
            P("section", None, "ha", "wa", None, None),
            P(None, "ha", "wa"),
        ),
        out_specs=P(None, "section", None, "ha", "wa", None, None),
        check_vma=False,
    )
```

```python
import functools

import jax
import jax.numpy as jnp
from jax import lax
from jax.experimental import pallas as pl
from jax.experimental.pallas import tpu as pltpu
from jax.sharding import PartitionSpec as P

HEAD_DIM = 128
HEADS_PER_CHUNK = 1
MESH = pl.DeviceIdType.MESH
F32 = jnp.float32
BF16 = jnp.bfloat16

Y_KV, Z_Q, EXT, CORNER, STAT, DQ, EXT_PART, CORNER_PART, Y_PART, OUT, KINDS = (
    0, 1, 3, 4, 5, 7, 9, 10, 11, 12, 13)

AHEAD_Y = 6
AHEAD_Q = 3, 3
AHEAD_E = 3, 3
CORNERS_AHEAD = 2
STAT_LAG = 2
FOLD_LAG = 4
LOW = -1e30
VMEM_KIB = 56000


def dot(a, b, contract):
    return lax.dot_general(a, b, ((contract[0], contract[1]), ((), ())), preferred_element_type=F32)


def merge(top, lse, mean, lse_other, mean_other):
    most = jnp.maximum(lse, lse_other)
    w, w_other = jnp.exp(lse - most), jnp.exp(lse_other - most)
    inv = 1.0 / (w + w_other)
    return jnp.exp(top - most) * inv, (w * mean + w_other * mean_other) * inv


def kernel(sizes, starts, q_in, kv_in, go_in, out, qg, kx, qz, load_sem, first_send, first_recv, first_sem, bias,
           bias_z, e_own, dp_own, st_own, e_z, dp_z, st_z, stat_send, stat_recv, acc, dqz_send, dqz_recv,
           pz_send, pz_recv, pc_recv, py_send, py_recv, own, total_q, total_kv, send_sem, recv_sem):
    n_sec, n_ha, n_wa, chunks, width = sizes
    _, grid_t, rows, cols, tok, _ = qg.shape
    per_col = grid_t * rows * tok
    per_key = grid_t * (rows + 1) * tok
    slots = e_own.shape[0]
    sec, ha, wa = lax.axis_index("section"), lax.axis_index("ha"), lax.axis_index("wa")
    before = lax.rem(sec + n_sec - 1, n_sec)
    after = lax.rem(sec + 1, n_sec)
    other = 1 - ha
    edge = other * (rows - 1)
    inner = rows - 1 - edge
    has = (wa > 0, wa < n_wa - 1)
    peer = (wa - 1, wa + 1)
    near = (0, cols - 1)
    rim = (wa == 0) | (wa == n_wa - 1)
    by_rim = (wa == 1, wa == n_wa - 2)
    scale = HEAD_DIM ** (-0.5)

    loads = [pltpu.make_async_copy(src, dst, load_sem.at[n]) for n, (src, dst) in enumerate(
        ((q_in, qg.at[0]), (go_in, qg.at[1]), (kv_in, kx.at[:, :, 0:rows, 0:cols])))]
    for load in loads:
        load.start()

    n_q = cols * per_col
    lane = lax.broadcasted_iota(jnp.int32, (1, n_q), 1)
    first = jnp.zeros((1, n_q), F32)
    for c in range(cols):
        for t in range(grid_t):
            for r in range(rows):
                tile = (c * grid_t + t) * rows + r
                first = jnp.where(lane // tok == tile, starts[r, c, t].astype(F32), first)
    first_send[...] = jnp.broadcast_to(first, first_send.shape)

    barrier = pltpu.get_barrier_semaphore()

    def greet(*device):
        pl.semaphore_signal(barrier, inc=1, device_id=device, device_id_type=MESH)

    greet(before, ha, wa)
    greet(after, ha, wa)
    greet(sec, other, wa)
    for side in (0, 1):
        @pl.when(has[side])
        def _():
            greet(sec, ha, peer[side])

        @pl.when(has[side] & (rim | by_rim[side]))
        def _():
            greet(sec, other, peer[side])

    sides_here = jnp.minimum(wa, 1) + jnp.minimum(n_wa - 1 - wa, 1)
    rims_here = jnp.where(rim, 1, by_rim[0].astype(jnp.int32) + by_rim[1].astype(jnp.int32))
    pl.semaphore_wait(barrier, 3 + sides_here + rims_here)

    def keys_move(c):
        return ((lax.rem(c, 5) == 2) | (lax.rem(c, 5) == 0)) & (c > 0) & (c < chunks - 2)

    def lanes(c):
        return pl.ds(pl.multiple_of(c * width, width), width)

    def within(j):
        return slice(j * HEAD_DIM, (j + 1) * HEAD_DIM)

    def channels(c, j):
        return pl.ds(pl.multiple_of(c * width + j * HEAD_DIM, HEAD_DIM), HEAD_DIM)

    def remote(src, dst, sent, arrived, c, device):
        return pltpu.make_async_remote_copy(
            src_ref=src, dst_ref=dst, send_sem=send_sem.at[sent, c], recv_sem=recv_sem.at[arrived, c],
            device_id=device, device_id_type=MESH)

    def y_kv(c):
        return remote(kx.at[:, :, edge, 0:cols, :, lanes(c)], kx.at[:, :, rows, 0:cols, :, lanes(c)],
                      Y_KV, Y_KV, c, (sec, other, wa))

    def z_q(side, c, both):
        at = slice(0, cols) if both else slice(near[side], near[side] + 1)
        return remote(qg.at[:, :, :, at, :, lanes(c)], qz.at[1 - side, :, :, :, at, :, lanes(c)],
                      Z_Q + side, Z_Q + 1 - side, c, (sec, ha, peer[side]))

    def ext(side, c):
        return remote(kx.at[:, :, 0:rows, near[side], :, lanes(c)], kx.at[:, :, 0:rows, cols, :, lanes(c)],
                      EXT, EXT, c, (sec, ha, peer[side]))

    def corner(side, c):
        return remote(kx.at[:, :, rows, near[side], :, lanes(c)], kx.at[:, :, rows, cols, :, lanes(c)],
                      CORNER, CORNER, c, (sec, ha, peer[side]))

    def stat(side, c, both):
        at = slice(0, cols if both else 1)
        return remote(stat_send.at[side, c, :, at], stat_recv.at[1 - side, c, :, at],
                      STAT + side, STAT + 1 - side, c, (sec, ha, peer[side]))

    def dq_back(side, c, both):
        col = near[1 - side]
        at = slice(0, cols) if both else slice(col, col + 1)
        return remote(dqz_send.at[side, :, :, at, :, lanes(c)], dqz_recv.at[1 - side, :, :, at, :, lanes(c)],
                      DQ + side, DQ + 1 - side, c, (sec, ha, peer[side]))

    def ext_part(side, c):
        return remote(pz_send.at[:, :, 0:rows, :, lanes(c)], pz_recv.at[:, :, :, :, lanes(c)],
                      EXT_PART, EXT_PART, c, (sec, ha, peer[side]))

    def corner_part(side, c):
        return remote(pz_send.at[:, :, rows, :, lanes(c)], pc_recv.at[:, :, :, lanes(c)],
                      CORNER_PART, CORNER_PART, c, (sec, other, peer[side]))

    def y_part(c):
        return remote(py_send.at[:, :, :, :, lanes(c)], py_recv.at[:, :, :, :, lanes(c)],
                      Y_PART, Y_PART, c, (sec, other, wa))

    def result(*at):
        return remote(own.at[at], out.at[at], OUT, OUT, 0, (before, ha, wa))

    def kv_row(row, c):
        return pl.ds(1, 2), slice(None), row, slice(None), slice(None), lanes(c)

    def if_(cond, action):
        pl.when(cond)(action)

    def leaving(c, action):
        moved = keys_move(c)
        for side in (0, 1):
            if_(has[side] & rim & jnp.logical_not(moved), lambda: action(side, True))
            if_(has[side] & jnp.logical_not(rim), lambda: action(side, False))

    def coming(c, action):
        moved = keys_move(c)
        for side in (0, 1):
            if_(by_rim[side] & jnp.logical_not(moved), lambda: action(side, True))
            if_(has[side] & jnp.logical_not(by_rim[side]), lambda: action(side, False))

    def exchanged(c, action):
        moved = keys_move(c)
        for side in (0, 1):
            wide = (rim | by_rim[side]) & jnp.logical_not(moved)
            if_(has[side] & wide, lambda: action(side, True))
            if_(has[side] & jnp.logical_not(wide), lambda: action(side, False))

    def keys_leave(c, action):
        for side in (0, 1):
            if_(by_rim[side] & keys_move(c), lambda: action(side))

    def keys_come(c, action):
        for side in (0, 1):
            if_(has[side] & rim & keys_move(c), lambda: action(side))

    def queries_send(c):
        leaving(c, lambda side, both: z_q(side, c, both).start())

    def keys_send(c):
        keys_leave(c, lambda side: ext(side, c).start())

    def passes_corner(c):
        return (by_rim[0] | by_rim[1]) & keys_move(c)

    def stage_corner(c):
        if_(passes_corner(c), lambda: y_kv(c).wait_recv())
        keys_leave(c, lambda side: corner(side, c).start())

    def block(ref, lead, col, ch, n):
        return ref[lead + (slice(None), slice(None), col, slice(None), ch)].reshape(n, HEAD_DIM)

    def joined(ref, lead, at, ch, n):
        return jnp.concatenate([block(ref, lead, col, ch, n) for col in at])

    def first_phase(k, v, qh, gh, bias_of, e_ref, dp_ref, st_ref):
        s = dot(k, qh, ((1,), (1,))) * scale
        s = (s.reshape(-1, per_key, s.shape[1]) + bias_of).reshape(s.shape)
        top = jnp.max(s, axis=0, keepdims=True)
        e = jnp.exp(s - top)
        dp = dot(v, gh, ((1,), (1,)))
        total = jnp.sum(e, axis=0, keepdims=True)
        lse = top + jnp.log(total)
        mean = jnp.sum(e * dp, axis=0, keepdims=True) / total
        e_ref[...] = e
        dp_ref[...] = dp
        st_ref[0:1] = top
        st_ref[1:2] = lse
        st_ref[2:3] = mean
        return lse, mean

    def second_phase(k, qh, gh, e_ref, dp_ref, st_ref, lse_other, mean_other):
        factor, delta = merge(st_ref[0:1], st_ref[1:2], st_ref[2:3], lse_other, mean_other)
        p = e_ref[...] * factor
        ds = (p * (dp_ref[...] - delta)).astype(BF16)
        return (dot(ds, qh, ((1,), (0,))) * scale, dot(p.astype(BF16), gh, ((1,), (0,))),
                dot(ds, k, ((0,), (0,))) * scale)

    def own_first(key_cols, c, j):
        ch, b = channels(c, j), lax.rem(c, slots // HEADS_PER_CHUNK) * HEADS_PER_CHUNK + j
        n = key_cols * per_key
        lse, mean = first_phase(
            joined(kx, (0,), range(key_cols), ch, per_key), joined(kx, (1,), range(key_cols), ch, per_key),
            joined(qg, (0,), range(cols), ch, per_col), joined(qg, (1,), range(cols), ch, per_col),
            bias[...], e_own.at[b, 0:n], dp_own.at[b, 0:n], st_own.at[b])
        for row, value in enumerate((lse, mean)):
            for side, order in ((0, (0, 1)), (1, (1, 0))):
                for n, col in enumerate(order):
                    stat_send[side, c, j, n, row:row + 1] = value[:, col * per_col:(col + 1) * per_col]

    def own_second(key_cols, c, j):
        ch, b = channels(c, j), lax.rem(c, slots // HEADS_PER_CHUNK) * HEADS_PER_CHUNK + j
        n = key_cols * per_key
        if key_cols > cols:
            lse_other, mean_other = LOW, 0.0
        else:
            def pick(row):
                at = slice(row, row + 1)
                low = jnp.where(has[0], stat_recv[0, c, j, 0, at], stat_recv[1, c, j, 1, at])
                high = jnp.where(has[1], stat_recv[1, c, j, 0, at], stat_recv[0, c, j, 1, at])
                return jnp.concatenate([low, high], axis=1)

            lse_other, mean_other = pick(2), pick(3)
        dk, dv, dqh = second_phase(
            joined(kx, (0,), range(key_cols), ch, per_key),
            joined(qg, (0,), range(cols), ch, per_col), joined(qg, (1,), range(cols), ch, per_col),
            e_own.at[b, 0:n], dp_own.at[b, 0:n], st_own.at[b], lse_other, mean_other)
        for i, grad in enumerate((dk, dv)):
            for col in range(key_cols):
                part = grad[col * per_key:(col + 1) * per_key].reshape(grid_t, rows + 1, tok, HEAD_DIM)
                if col < cols:
                    acc[i, :, :, col, :, within(j)] = part
                else:
                    pz_send[i, :, :, :, ch] = part.astype(BF16)
        for col in range(cols):
            part = dqh[col * per_col:(col + 1) * per_col].astype(BF16)
            own[0, :, :, col, :, ch] = part.reshape(grid_t, rows, tok, HEAD_DIM)

    def columns(side, both):
        return (near[1 - side], near[side]) if both else (near[1 - side],)

    def z_first(side, both, c, j):
        ch, b = channels(c, j), lax.rem(c, slots // HEADS_PER_CHUNK) * HEADS_PER_CHUNK + j
        at = columns(side, both)
        n = len(at) * per_col
        lse, mean = first_phase(
            block(kx, (0,), near[side], ch, per_key), block(kx, (1,), near[side], ch, per_key),
            joined(qz, (side, 0), at, ch, per_col), joined(qz, (side, 1), at, ch, per_col),
            bias_z[side, :, 0:n], e_z.at[side, b, :, 0:n], dp_z.at[side, b, :, 0:n], st_z.at[side, b, :, 0:n])
        for row, value in ((2, lse), (3, mean)):
            for m in range(len(at)):
                stat_send[side, c, j, m, row:row + 1] = value[:, m * per_col:(m + 1) * per_col]

    def z_second(side, both, c, j):
        ch, b = channels(c, j), lax.rem(c, slots // HEADS_PER_CHUNK) * HEADS_PER_CHUNK + j
        at = columns(side, both)
        n = len(at) * per_col
        dk, dv, dqh = second_phase(
            block(kx, (0,), near[side], ch, per_key),
            joined(qz, (side, 0), at, ch, per_col), joined(qz, (side, 1), at, ch, per_col),
            e_z.at[side, b, :, 0:n], dp_z.at[side, b, :, 0:n], st_z.at[side, b, :, 0:n],
            *(jnp.concatenate([stat_recv[side, c, j, m, row:row + 1] for m in range(len(at))], axis=1)
              for row in (0, 1)))
        for i, grad in enumerate((dk, dv)):
            acc[i, :, :, near[side], :, within(j)] += grad.reshape(grid_t, rows + 1, tok, HEAD_DIM)
        for m, col in enumerate(at):
            part = dqh[m * per_col:(m + 1) * per_col].astype(BF16)
            dqz_send[side, :, :, col, :, ch] = part.reshape(grid_t, rows, tok, HEAD_DIM)

    def heads(action):
        for j in range(HEADS_PER_CHUNK):
            action(j)

    def stage_first(c):
        if_(jnp.logical_not(passes_corner(c)), lambda: y_kv(c).wait_recv())

        def arrive(side):
            ext(1 - side, c).wait_recv()
            corner(1 - side, c).wait_recv()

        keys_come(c, arrive)
        far = rim & keys_move(c)
        if_(far, lambda: heads(lambda j: own_first(cols + 1, c, j)))
        if_(jnp.logical_not(far), lambda: heads(lambda j: own_first(cols, c, j)))

        def from_side(side, both):
            z_q(1 - side, c, both).wait_recv()
            heads(lambda j: z_first(side, both, c, j))

        coming(c, from_side)
        exchanged(c, lambda side, both: stat(side, c, both).start())

    def stage_second(c):
        exchanged(c, lambda side, both: stat(1 - side, c, both).wait_recv())
        far = rim & keys_move(c)
        if_(far, lambda: heads(lambda j: own_second(cols + 1, c, j)))
        if_(jnp.logical_not(far), lambda: heads(lambda j: own_second(cols, c, j)))

        def extra(side):
            ext_part(side, c).start()
            corner_part(side, c).start()

        keys_come(c, extra)

        def from_side(side, both):
            heads(lambda j: z_second(side, both, c, j))
            dq_back(side, c, both).start()

        coming(c, from_side)
        ch = lanes(c)
        py_send[:, :, :, :, ch] = acc[:, :, rows].astype(BF16)
        y_part(c).start()
        own[1:3, :, :, :, :, ch] = acc[:, :, 0:rows].astype(BF16)
        if_(jnp.logical_not(passes_corner(c)), lambda: result(*kv_row(inner, c)).start())

    def sent(c):
        y_kv(c).wait_send()
        leaving(c, lambda side, both: z_q(side, c, both).wait_send())

        def keys_sent(side):
            ext(side, c).wait_send()
            corner(side, c).wait_send()

        keys_leave(c, keys_sent)

        def extra_sent(side):
            ext_part(side, c).wait_send()
            corner_part(side, c).wait_send()

        keys_come(c, extra_sent)
        exchanged(c, lambda side, both: stat(side, c, both).wait_send())
        coming(c, lambda side, both: dq_back(side, c, both).wait_send())
        y_part(c).wait_send()

    def stage_fold(c):
        ch = lanes(c)
        y_part(c).wait_recv()
        total_kv[...] = own[1:3, :, edge, :, :, ch].astype(F32) + py_recv[:, :, :, :, ch].astype(F32)

        def fold(side):
            ext_part(1 - side, c).wait_recv()
            corner_part(1 - side, c).wait_recv()
            total_kv[:, :, near[side]] += (
                pz_recv[:, :, edge, :, ch].astype(F32) + pc_recv[:, :, :, ch].astype(F32))
            own[1:3, :, inner, near[side], :, ch] = (
                own[1:3, :, inner, near[side], :, ch].astype(F32) + pz_recv[:, :, inner, :, ch].astype(F32)).astype(BF16)
            result(*kv_row(inner, c)).start()

        keys_leave(c, fold)
        own[1:3, :, edge, :, :, ch] = total_kv[...].astype(BF16)
        result(*kv_row(edge, c)).start()
        total_q[...] = own[0, :, :, :, :, ch].astype(F32)

        def back(side, both):
            dq_back(1 - side, c, both).wait_recv()
            for col in (range(cols) if both else (near[side],)):
                total_q[:, :, col] += dqz_recv[side, :, :, col, :, ch].astype(F32)

        leaving(c, back)
        own[0, :, :, :, :, ch] = total_q[...].astype(BF16)
        result(0, slice(None), slice(None), slice(None), slice(None), ch).start()
        sent(c)

    def first_copy(side):
        return pltpu.make_async_remote_copy(
            src_ref=first_send, dst_ref=first_recv.at[1 - side], send_sem=first_sem.at[0, side],
            recv_sem=first_sem.at[1, 1 - side], device_id=(sec, ha, peer[side]), device_id_type=MESH)

    for side in (0, 1):
        if_(has[side], lambda: first_copy(side).start())

    for load in loads:
        load.wait()
    ahead_q, ahead_e = (jnp.where(lax.rem(sec, 2) == 0, a, b) for a, b in (AHEAD_Q, AHEAD_E))
    for c in range(max(AHEAD_Y, *AHEAD_Q, *AHEAD_E)):
        if c < AHEAD_Y:
            y_kv(c).start()
        if_(c < ahead_q, lambda: queries_send(c))
        if_(c < ahead_e, lambda: keys_send(c))

    def window(ref, begin):
        per_t = (rows + 1) * tok
        for t in range(grid_t):
            seen = (begin <= t) & (begin + 2 >= t)
            row = jnp.where(seen, 0.0, LOW).astype(F32)
            ref[t * per_t:(t + 1) * per_t, :] = jnp.broadcast_to(row, (per_t, n_q))

    window(bias, first)
    for c in range(CORNERS_AHEAD):
        stage_corner(c)
    for side in (0, 1):
        def _(side=side):
            first_copy(1 - side).wait_recv()
            begin = jnp.concatenate(
                [first_recv[side, 0:1, col * per_col:(col + 1) * per_col] for col in columns(side, True)], axis=1)
            window(bias_z.at[side], begin)
        if_(has[side], _)

    def step(i, carry):
        if_(i + AHEAD_Y < chunks, lambda: y_kv(i + AHEAD_Y).start())
        if_(i + ahead_q < chunks, lambda: queries_send(i + ahead_q))
        if_(i + ahead_e < chunks, lambda: keys_send(i + ahead_e))
        if_(i + CORNERS_AHEAD < chunks, lambda: stage_corner(i + CORNERS_AHEAD))
        if_(i < chunks, lambda: stage_first(i))
        if_((i >= STAT_LAG) & (i < chunks + STAT_LAG), lambda: stage_second(i - STAT_LAG))
        if_(i >= FOLD_LAG, lambda: stage_fold(i - FOLD_LAG))
        return carry

    lax.fori_loop(0, chunks + FOLD_LAG, step, 0)
    result().wait()
    for side in (0, 1):
        if_(has[side], lambda: first_copy(side).wait_send())


def local(mesh_sizes, queries, keys_values, grad_out, time_start):
    n_sec, n_ha, n_wa = mesh_sizes
    q, kv, go = queries[0], keys_values[:, 0], grad_out[0]
    grid_t, rows, cols, tok, channels = q.shape
    assert n_ha == 2 and rows == 2 and cols == 2 and n_wa >= 4 and n_sec >= 2
    width = HEADS_PER_CHUNK * HEAD_DIM
    assert channels % width == 0
    chunks = channels // width
    assert chunks >= max(AHEAD_Y, *AHEAD_Q, *AHEAD_E) and AHEAD_Y >= CORNERS_AHEAD
    per_col, per_key = grid_t * rows * tok, grid_t * (rows + 1) * tok
    n_q = cols * per_col
    slots = (STAT_LAG + 1) * HEADS_PER_CHUNK
    stay = pl.BlockSpec(memory_space=pl.ANY)
    vmem = pltpu.VMEM
    out = pl.pallas_call(
        functools.partial(kernel, (n_sec, n_ha, n_wa, chunks, width)),
        out_shape=pltpu.VMEM((3,) + q.shape, BF16),
        in_specs=[pl.BlockSpec(memory_space=pltpu.SMEM), stay, stay, stay],
        out_specs=pl.BlockSpec(memory_space=pltpu.VMEM),
        scratch_shapes=[
            vmem((2,) + q.shape, BF16),
            vmem((2, grid_t, rows + 1, cols + 1, tok, channels), BF16),
            vmem((2, 2) + q.shape, BF16),
            pltpu.SemaphoreType.DMA((3,)),
            vmem((8, n_q), F32),
            vmem((2, 8, n_q), F32),
            pltpu.SemaphoreType.DMA((2, 2)),
            vmem((per_key, n_q), F32),
            vmem((2, per_key, n_q), F32),
            vmem((slots, (cols + 1) * per_key, n_q), F32),
            vmem((slots, (cols + 1) * per_key, n_q), F32),
            vmem((slots, 8, n_q), F32),
            vmem((2, slots, per_key, n_q), F32),
            vmem((2, slots, per_key, n_q), F32),
            vmem((2, slots, 8, n_q), F32),
            vmem((2, chunks, HEADS_PER_CHUNK, cols, 4, per_col), F32),
            vmem((2, chunks, HEADS_PER_CHUNK, cols, 4, per_col), F32),
            vmem((2, grid_t, rows + 1, cols, tok, width), F32),
            vmem((2,) + q.shape, BF16),
            vmem((2,) + q.shape, BF16),
            vmem((2, grid_t, rows + 1, tok, channels), BF16),
            vmem((2, grid_t, rows, tok, channels), BF16),
            vmem((2, grid_t, tok, channels), BF16),
            vmem((2, grid_t, cols, tok, channels), BF16),
            vmem((2, grid_t, cols, tok, channels), BF16),
            vmem((3,) + q.shape, BF16),
            vmem((grid_t, rows, cols, tok, width), F32),
            vmem((2, grid_t, cols, tok, width), F32),
            pltpu.SemaphoreType.DMA((KINDS, chunks)),
            pltpu.SemaphoreType.DMA((KINDS, chunks)),
        ],
        compiler_params=pltpu.CompilerParams(
            collective_id=0, has_side_effects=True, vmem_limit_bytes=VMEM_KIB * 1024
        ),
    )(time_start.transpose(1, 2, 0), q, kv, go)
    return out[:, None]


def solution(mesh):
    sizes = (mesh.shape["section"], mesh.shape["ha"], mesh.shape["wa"])
    return jax.shard_map(
        functools.partial(local, sizes),
        mesh=mesh,
        in_specs=(
            P("section", None, "ha", "wa", None, None),
            P(None, "section", None, "ha", "wa", None, None),
            P("section", None, "ha", "wa", None, None),
            P(None, "ha", "wa"),
        ),
        out_specs=P(None, "section", None, "ha", "wa", None, None),
        check_vma=False,
    )
```

```python
import functools

import jax
import jax.numpy as jnp
from jax import lax
from jax.experimental import pallas as pl
from jax.experimental.pallas import tpu as pltpu
from jax.sharding import PartitionSpec as P

HEAD_DIM = 128
HEADS_PER_CHUNK = 1
MESH = pl.DeviceIdType.MESH
F32 = jnp.float32
BF16 = jnp.bfloat16

Y_KV, Z_Q, EXT, CORNER, STAT, DQ, EXT_INNER, EXT_EDGE, CORNER_PART, Y_PART, OUT, SHIFT, KINDS = (
    0, 1, 3, 4, 5, 7, 9, 10, 11, 12, 13, 14, 15)

AHEAD_Y = 6
AHEAD_Q = 3, 3
AHEAD_E = 3, 3
CORNERS_AHEAD = 2
STAT_LAG = 2
MERGE_LAG = 3
FOLD_LAG = 5
SHIFTED = 6
LOW = -1e30
VMEM_KIB = 56000


def dot(a, b, contract):
    return lax.dot_general(a, b, ((contract[0], contract[1]), ((), ())), preferred_element_type=F32)


def merge(top, lse, mean, lse_other, mean_other):
    most = jnp.maximum(lse, lse_other)
    w, w_other = jnp.exp(lse - most), jnp.exp(lse_other - most)
    inv = 1.0 / (w + w_other)
    return jnp.exp(top - most) * inv, (w * mean + w_other * mean_other) * inv


def kernel(sizes, starts, q_in, kv_in, go_in, out, qg, kx, qz, load_sem, first_send, first_recv, first_sem, bias,
           bias_z, e_own, dp_own, st_own, e_z, dp_z, st_z, stat_send, stat_recv, acc, dqz_send, dqz_recv,
           pz_send, pz_recv, pc_recv, py_send, py_recv, own, total_q, total_kv, send_sem, recv_sem):
    n_sec, n_ha, n_wa, chunks, width = sizes
    _, grid_t, rows, cols, tok, _ = qg.shape
    per_col = grid_t * rows * tok
    per_key = grid_t * (rows + 1) * tok
    slots = e_own.shape[0]
    sec, ha, wa = lax.axis_index("section"), lax.axis_index("ha"), lax.axis_index("wa")
    before = lax.rem(sec + n_sec - 1, n_sec)
    after = lax.rem(sec + 1, n_sec)
    other = 1 - ha
    edge = other * (rows - 1)
    inner = rows - 1 - edge
    has = (wa > 0, wa < n_wa - 1)
    peer = (wa - 1, wa + 1)
    near = (0, cols - 1)
    rim = (wa == 0) | (wa == n_wa - 1)
    by_rim = (wa == 1, wa == n_wa - 2)
    scale = HEAD_DIM ** (-0.5)

    staying = chunks - SHIFTED
    kept, moved_on = slice(0, staying * width), slice(staying * width, chunks * width)

    def held(at):
        return ((q_in, qg.at[0, :, :, :, :, at]), (go_in, qg.at[1, :, :, :, :, at]),
                (kv_in, kx.at[:, :, 0:rows, 0:cols, :, at]))

    loads = [pltpu.make_async_copy(src.at[(slice(None),) * (len(src.shape) - 1) + (kept,)], dst, load_sem.at[n])
             for n, (src, dst) in enumerate(held(kept))]
    for load in loads:
        load.start()

    n_q = cols * per_col
    lane = lax.broadcasted_iota(jnp.int32, (1, n_q), 1)
    first = jnp.zeros((1, n_q), F32)
    for c in range(cols):
        for t in range(grid_t):
            for r in range(rows):
                tile = (c * grid_t + t) * rows + r
                first = jnp.where(lane // tok == tile, starts[r, c, t].astype(F32), first)
    first_send[...] = jnp.broadcast_to(first, first_send.shape)

    barrier = pltpu.get_barrier_semaphore()

    def greet(*device):
        pl.semaphore_signal(barrier, inc=1, device_id=device, device_id_type=MESH)

    greet(before, ha, wa)
    greet(after, ha, wa)
    greet(sec, other, wa)
    for side in (0, 1):
        @pl.when(has[side])
        def _():
            greet(sec, ha, peer[side])

    sides_here = jnp.minimum(wa, 1) + jnp.minimum(n_wa - 1 - wa, 1)
    pl.semaphore_wait(barrier, 3 + sides_here)

    def keys_move(c):
        return (lax.rem(c, 3) == 2) & (c < chunks - 2)

    def lanes(c):
        return pl.ds(pl.multiple_of(c * width, width), width)

    def within(j):
        return slice(j * HEAD_DIM, (j + 1) * HEAD_DIM)

    def channels(c, j):
        return pl.ds(pl.multiple_of(c * width + j * HEAD_DIM, HEAD_DIM), HEAD_DIM)

    def remote(src, dst, sent, arrived, c, device):
        return pltpu.make_async_remote_copy(
            src_ref=src, dst_ref=dst, send_sem=send_sem.at[sent, c], recv_sem=recv_sem.at[arrived, c],
            device_id=device, device_id_type=MESH)

    shifts = [remote(src.at[(slice(None),) * (len(src.shape) - 1) + (moved_on,)], dst, SHIFT, SHIFT, n, (before, ha, wa))
              for n, (src, dst) in enumerate(held(moved_on))]

    def y_kv(c):
        return remote(kx.at[:, :, edge, 0:cols, :, lanes(c)], kx.at[:, :, rows, 0:cols, :, lanes(c)],
                      Y_KV, Y_KV, c, (sec, other, wa))

    def z_q(side, c, both):
        at = slice(0, cols) if both else slice(near[side], near[side] + 1)
        return remote(qg.at[:, :, :, at, :, lanes(c)], qz.at[1 - side, :, :, :, at, :, lanes(c)],
                      Z_Q + side, Z_Q + 1 - side, c, (sec, ha, peer[side]))

    def ext(side, c):
        return remote(kx.at[:, :, 0:rows, near[side], :, lanes(c)], kx.at[:, :, 0:rows, cols, :, lanes(c)],
                      EXT, EXT, c, (sec, ha, peer[side]))

    def corner(side, c):
        return remote(kx.at[:, :, rows, near[side], :, lanes(c)], kx.at[:, :, rows, cols, :, lanes(c)],
                      CORNER, CORNER, c, (sec, ha, peer[side]))

    def stat(side, c, both):
        at = slice(0, cols if both else 1)
        return remote(stat_send.at[side, c, :, at], stat_recv.at[1 - side, c, :, at],
                      STAT + side, STAT + 1 - side, c, (sec, ha, peer[side]))

    def dq_back(side, c, both):
        col = near[1 - side]
        at = slice(0, cols) if both else slice(col, col + 1)
        return remote(dqz_send.at[side, :, :, at, :, lanes(c)], dqz_recv.at[1 - side, :, :, at, :, lanes(c)],
                      DQ + side, DQ + 1 - side, c, (sec, ha, peer[side]))

    def ext_inner(side, c):
        return remote(pz_send.at[:, :, inner, :, lanes(c)], pz_recv.at[:, :, inner, :, lanes(c)],
                      EXT_INNER, EXT_INNER, c, (sec, ha, peer[side]))

    def ext_edge(side, c):
        return remote(pz_send.at[:, :, edge, :, lanes(c)], pz_recv.at[:, :, edge, :, lanes(c)],
                      EXT_EDGE, EXT_EDGE, c, (sec, ha, peer[side]))

    def corner_part(c):
        return remote(pz_send.at[:, :, rows, :, lanes(c)], pc_recv.at[:, :, :, lanes(c)],
                      CORNER_PART, CORNER_PART, c, (sec, other, wa))

    def y_part(c):
        return remote(py_send.at[:, :, :, :, lanes(c)], py_recv.at[:, :, :, :, lanes(c)],
                      Y_PART, Y_PART, c, (sec, other, wa))

    def result(*at):
        return remote(own.at[at], out.at[at], OUT, OUT, 0, (before, ha, wa))

    def kv_row(row, c):
        return pl.ds(1, 2), slice(None), row, slice(None), slice(None), lanes(c)

    def if_(cond, action):
        pl.when(cond)(action)

    def leaving(c, action):
        moved = keys_move(c)
        for side in (0, 1):
            if_(has[side] & rim & jnp.logical_not(moved), lambda: action(side, True))
            if_(has[side] & jnp.logical_not(rim), lambda: action(side, False))

    def coming(c, action):
        moved = keys_move(c)
        for side in (0, 1):
            if_(by_rim[side] & jnp.logical_not(moved), lambda: action(side, True))
            if_(has[side] & jnp.logical_not(by_rim[side]), lambda: action(side, False))

    def exchanged(c, action):
        moved = keys_move(c)
        for side in (0, 1):
            wide = (rim | by_rim[side]) & jnp.logical_not(moved)
            if_(has[side] & wide, lambda: action(side, True))
            if_(has[side] & jnp.logical_not(wide), lambda: action(side, False))

    def keys_leave(c, action):
        for side in (0, 1):
            if_(by_rim[side] & keys_move(c), lambda: action(side))

    def keys_come(c, action):
        for side in (0, 1):
            if_(has[side] & rim & keys_move(c), lambda: action(side))

    def queries_send(c):
        leaving(c, lambda side, both: z_q(side, c, both).start())

    def keys_send(c):
        keys_leave(c, lambda side: ext(side, c).start())

    def passes_corner(c):
        return (by_rim[0] | by_rim[1]) & keys_move(c)

    def stage_corner(c):
        if_(passes_corner(c), lambda: y_kv(c).wait_recv())
        keys_leave(c, lambda side: corner(side, c).start())

    def block(ref, lead, col, ch, n):
        return ref[lead + (slice(None), slice(None), col, slice(None), ch)].reshape(n, HEAD_DIM)

    def joined(ref, lead, at, ch, n):
        return jnp.concatenate([block(ref, lead, col, ch, n) for col in at])

    def first_phase(k, v, qh, gh, bias_of, e_ref, dp_ref, st_ref):
        s = dot(k, qh, ((1,), (1,))) * scale
        s = (s.reshape(-1, per_key, s.shape[1]) + bias_of).reshape(s.shape)
        top = jnp.max(s, axis=0, keepdims=True)
        e = jnp.exp(s - top)
        dp = dot(v, gh, ((1,), (1,)))
        total = jnp.sum(e, axis=0, keepdims=True)
        lse = top + jnp.log(total)
        mean = jnp.sum(e * dp, axis=0, keepdims=True) / total
        e_ref[...] = e
        dp_ref[...] = dp
        st_ref[0:1] = top
        st_ref[1:2] = lse
        st_ref[2:3] = mean
        return lse, mean

    def second_phase(k, qh, gh, e_ref, dp_ref, st_ref, lse_other, mean_other):
        factor, delta = merge(st_ref[0:1], st_ref[1:2], st_ref[2:3], lse_other, mean_other)
        p = e_ref[...] * factor
        ds = (p * (dp_ref[...] - delta)).astype(BF16)
        return (dot(ds, qh, ((1,), (0,))) * scale, dot(p.astype(BF16), gh, ((1,), (0,))),
                dot(ds, k, ((0,), (0,))) * scale)

    def own_first(key_cols, c, j):
        ch, b = channels(c, j), lax.rem(c, slots // HEADS_PER_CHUNK) * HEADS_PER_CHUNK + j
        n = key_cols * per_key
        lse, mean = first_phase(
            joined(kx, (0,), range(key_cols), ch, per_key), joined(kx, (1,), range(key_cols), ch, per_key),
            joined(qg, (0,), range(cols), ch, per_col), joined(qg, (1,), range(cols), ch, per_col),
            bias[...], e_own.at[b, 0:n], dp_own.at[b, 0:n], st_own.at[b])
        for row, value in enumerate((lse, mean)):
            for side, order in ((0, (0, 1)), (1, (1, 0))):
                for n, col in enumerate(order):
                    stat_send[side, c, j, n, row:row + 1] = value[:, col * per_col:(col + 1) * per_col]

    def own_second(key_cols, c, j):
        ch, b = channels(c, j), lax.rem(c, slots // HEADS_PER_CHUNK) * HEADS_PER_CHUNK + j
        n = key_cols * per_key
        if key_cols > cols:
            lse_other, mean_other = LOW, 0.0
        else:
            def pick(row):
                at = slice(row, row + 1)
                low = jnp.where(has[0], stat_recv[0, c, j, 0, at], stat_recv[1, c, j, 1, at])
                high = jnp.where(has[1], stat_recv[1, c, j, 0, at], stat_recv[0, c, j, 1, at])
                return jnp.concatenate([low, high], axis=1)

            lse_other, mean_other = pick(2), pick(3)
        dk, dv, dqh = second_phase(
            joined(kx, (0,), range(key_cols), ch, per_key),
            joined(qg, (0,), range(cols), ch, per_col), joined(qg, (1,), range(cols), ch, per_col),
            e_own.at[b, 0:n], dp_own.at[b, 0:n], st_own.at[b], lse_other, mean_other)
        for i, grad in enumerate((dk, dv)):
            for col in range(key_cols):
                part = grad[col * per_key:(col + 1) * per_key].reshape(grid_t, rows + 1, tok, HEAD_DIM)
                if col < cols:
                    acc[i, :, :, col, :, within(j)] = part
                else:
                    pz_send[i, :, :, :, ch] = part.astype(BF16)
        for col in range(cols):
            part = dqh[col * per_col:(col + 1) * per_col].astype(BF16)
            own[0, :, :, col, :, ch] = part.reshape(grid_t, rows, tok, HEAD_DIM)

    def columns(side, both):
        return (near[1 - side], near[side]) if both else (near[1 - side],)

    def z_first(side, both, c, j):
        ch, b = channels(c, j), lax.rem(c, slots // HEADS_PER_CHUNK) * HEADS_PER_CHUNK + j
        at = columns(side, both)
        n = len(at) * per_col
        lse, mean = first_phase(
            block(kx, (0,), near[side], ch, per_key), block(kx, (1,), near[side], ch, per_key),
            joined(qz, (side, 0), at, ch, per_col), joined(qz, (side, 1), at, ch, per_col),
            bias_z[side, :, 0:n], e_z.at[side, b, :, 0:n], dp_z.at[side, b, :, 0:n], st_z.at[side, b, :, 0:n])
        for row, value in ((2, lse), (3, mean)):
            for m in range(len(at)):
                stat_send[side, c, j, m, row:row + 1] = value[:, m * per_col:(m + 1) * per_col]

    def z_second(side, both, c, j):
        ch, b = channels(c, j), lax.rem(c, slots // HEADS_PER_CHUNK) * HEADS_PER_CHUNK + j
        at = columns(side, both)
        n = len(at) * per_col
        dk, dv, dqh = second_phase(
            block(kx, (0,), near[side], ch, per_key),
            joined(qz, (side, 0), at, ch, per_col), joined(qz, (side, 1), at, ch, per_col),
            e_z.at[side, b, :, 0:n], dp_z.at[side, b, :, 0:n], st_z.at[side, b, :, 0:n],
            *(jnp.concatenate([stat_recv[side, c, j, m, row:row + 1] for m in range(len(at))], axis=1)
              for row in (0, 1)))
        for i, grad in enumerate((dk, dv)):
            acc[i, :, :, near[side], :, within(j)] += grad.reshape(grid_t, rows + 1, tok, HEAD_DIM)
        for m, col in enumerate(at):
            part = dqh[m * per_col:(m + 1) * per_col].astype(BF16)
            dqz_send[side, :, :, col, :, ch] = part.reshape(grid_t, rows, tok, HEAD_DIM)

    def heads(action):
        for j in range(HEADS_PER_CHUNK):
            action(j)

    def stage_first(c):
        if_(jnp.logical_not(passes_corner(c)), lambda: y_kv(c).wait_recv())

        def arrive(side):
            ext(1 - side, c).wait_recv()
            corner(1 - side, c).wait_recv()

        keys_come(c, arrive)
        far = rim & keys_move(c)
        if_(far, lambda: heads(lambda j: own_first(cols + 1, c, j)))
        if_(jnp.logical_not(far), lambda: heads(lambda j: own_first(cols, c, j)))

        def from_side(side, both):
            z_q(1 - side, c, both).wait_recv()
            heads(lambda j: z_first(side, both, c, j))

        coming(c, from_side)
        exchanged(c, lambda side, both: stat(side, c, both).start())

    def stage_second(c):
        exchanged(c, lambda side, both: stat(1 - side, c, both).wait_recv())
        far = rim & keys_move(c)
        if_(far, lambda: heads(lambda j: own_second(cols + 1, c, j)))
        if_(jnp.logical_not(far), lambda: heads(lambda j: own_second(cols, c, j)))

        def extra(side):
            ext_inner(side, c).start()
            corner_part(c).start()

        keys_come(c, extra)

        def from_side(side, both):
            heads(lambda j: z_second(side, both, c, j))
            dq_back(side, c, both).start()

        coming(c, from_side)
        ch = lanes(c)
        py_send[:, :, :, :, ch] = acc[:, :, rows].astype(BF16)
        y_part(c).start()
        own[1:3, :, :, :, :, ch] = acc[:, :, 0:rows].astype(BF16)
        if_(jnp.logical_not(passes_corner(c)) & (c < staying), lambda: result(*kv_row(inner, c)).start())

    def sent(c):
        y_kv(c).wait_send()
        leaving(c, lambda side, both: z_q(side, c, both).wait_send())

        def keys_sent(side):
            ext(side, c).wait_send()
            corner(side, c).wait_send()

        keys_leave(c, keys_sent)

        def extra_sent(side):
            ext_inner(side, c).wait_send()
            ext_edge(side, c).wait_send()
            corner_part(c).wait_send()

        keys_come(c, extra_sent)
        exchanged(c, lambda side, both: stat(side, c, both).wait_send())
        coming(c, lambda side, both: dq_back(side, c, both).wait_send())
        y_part(c).wait_send()

    def stage_merge(c):
        ch = lanes(c)

        def merged(side):
            corner_part(c).wait_recv()
            pz_send[:, :, edge, :, ch] = (
                pz_send[:, :, edge, :, ch].astype(F32) + pc_recv[:, :, :, ch].astype(F32)).astype(BF16)
            ext_edge(side, c).start()

        keys_come(c, merged)

    def stage_fold(c):
        ch = lanes(c)
        y_part(c).wait_recv()
        total_kv[...] = own[1:3, :, edge, :, :, ch].astype(F32) + py_recv[:, :, :, :, ch].astype(F32)

        def fold(side):
            ext_edge(1 - side, c).wait_recv()
            total_kv[:, :, near[side]] += pz_recv[:, :, edge, :, ch].astype(F32)
            ext_inner(1 - side, c).wait_recv()
            own[1:3, :, inner, near[side], :, ch] = (
                own[1:3, :, inner, near[side], :, ch].astype(F32) + pz_recv[:, :, inner, :, ch].astype(F32)).astype(BF16)
            if_(c < staying, lambda: result(*kv_row(inner, c)).start())

        keys_leave(c, fold)
        own[1:3, :, edge, :, :, ch] = total_kv[...].astype(BF16)
        if_(c < staying, lambda: result(*kv_row(edge, c)).start())
        total_q[...] = own[0, :, :, :, :, ch].astype(F32)

        def back(side, both):
            dq_back(1 - side, c, both).wait_recv()
            for col in (range(cols) if both else (near[side],)):
                total_q[:, :, col] += dqz_recv[side, :, :, col, :, ch].astype(F32)

        leaving(c, back)

        def leave():
            own[0, :, :, :, :, ch] = total_q[...].astype(BF16)
            result(0, slice(None), slice(None), slice(None), slice(None), ch).start()

        def stay():
            out[0, :, :, :, :, ch] = total_q[...].astype(BF16)
            out[1:3, :, :, :, :, ch] = own[1:3, :, :, :, :, ch]

        if_(c < staying, leave)
        if_(c >= staying, stay)
        sent(c)

    def first_copy(side):
        return pltpu.make_async_remote_copy(
            src_ref=first_send, dst_ref=first_recv.at[1 - side], send_sem=first_sem.at[0, side],
            recv_sem=first_sem.at[1, 1 - side], device_id=(sec, ha, peer[side]), device_id_type=MESH)

    for side in (0, 1):
        if_(has[side], lambda: first_copy(side).start())

    for shift in shifts:
        shift.start()
    for load in loads:
        load.wait()
    ahead_q, ahead_e = (jnp.where(lax.rem(sec, 2) == 0, a, b) for a, b in (AHEAD_Q, AHEAD_E))
    for c in range(max(AHEAD_Y, *AHEAD_Q, *AHEAD_E)):
        if c < AHEAD_Y:
            y_kv(c).start()
        if_(c < ahead_q, lambda: queries_send(c))
        if_(c < ahead_e, lambda: keys_send(c))

    def window(ref, begin):
        per_t = (rows + 1) * tok
        for t in range(grid_t):
            seen = (begin <= t) & (begin + 2 >= t)
            row = jnp.where(seen, 0.0, LOW).astype(F32)
            ref[t * per_t:(t + 1) * per_t, :] = jnp.broadcast_to(row, (per_t, n_q))

    window(bias, first)
    for c in range(CORNERS_AHEAD):
        stage_corner(c)
    for side in (0, 1):
        def _(side=side):
            first_copy(1 - side).wait_recv()
            begin = jnp.concatenate(
                [first_recv[side, 0:1, col * per_col:(col + 1) * per_col] for col in columns(side, True)], axis=1)
            window(bias_z.at[side], begin)
        if_(has[side], _)

    def step(i, carry):
        def arrived():
            for shift in shifts:
                shift.wait_recv()

        if_(i + AHEAD_Y == staying, arrived)
        if_(i + AHEAD_Y < chunks, lambda: y_kv(i + AHEAD_Y).start())
        if_(i + ahead_q < chunks, lambda: queries_send(i + ahead_q))
        if_(i + ahead_e < chunks, lambda: keys_send(i + ahead_e))
        if_(i + CORNERS_AHEAD < chunks, lambda: stage_corner(i + CORNERS_AHEAD))
        if_(i < chunks, lambda: stage_first(i))
        if_((i >= STAT_LAG) & (i < chunks + STAT_LAG), lambda: stage_second(i - STAT_LAG))
        if_((i >= MERGE_LAG) & (i < chunks + MERGE_LAG), lambda: stage_merge(i - MERGE_LAG))
        if_(i >= FOLD_LAG, lambda: stage_fold(i - FOLD_LAG))
        return carry

    lax.fori_loop(0, chunks + FOLD_LAG, step, 0)
    result(slice(None), slice(None), slice(None), slice(None), slice(None), kept).wait()
    for shift in shifts:
        shift.wait_send()
    for side in (0, 1):
        if_(has[side], lambda: first_copy(side).wait_send())


def local(mesh_sizes, queries, keys_values, grad_out, time_start):
    n_sec, n_ha, n_wa = mesh_sizes
    q, kv, go = queries[0], keys_values[:, 0], grad_out[0]
    grid_t, rows, cols, tok, channels = q.shape
    assert n_ha == 2 and rows == 2 and cols == 2 and n_wa >= 4 and n_sec >= 2
    width = HEADS_PER_CHUNK * HEAD_DIM
    assert channels % width == 0
    chunks = channels // width
    assert chunks >= max(AHEAD_Y, *AHEAD_Q, *AHEAD_E) and AHEAD_Y >= CORNERS_AHEAD
    assert AHEAD_Y >= max(*AHEAD_Q, *AHEAD_E) and chunks - SHIFTED >= AHEAD_Y and SHIFTED > 0
    per_col, per_key = grid_t * rows * tok, grid_t * (rows + 1) * tok
    n_q = cols * per_col
    slots = (STAT_LAG + 1) * HEADS_PER_CHUNK
    stay = pl.BlockSpec(memory_space=pl.ANY)
    vmem = pltpu.VMEM
    out = pl.pallas_call(
        functools.partial(kernel, (n_sec, n_ha, n_wa, chunks, width)),
        out_shape=pltpu.VMEM((3,) + q.shape, BF16),
        in_specs=[pl.BlockSpec(memory_space=pltpu.SMEM), stay, stay, stay],
        out_specs=pl.BlockSpec(memory_space=pltpu.VMEM),
        scratch_shapes=[
            vmem((2,) + q.shape, BF16),
            vmem((2, grid_t, rows + 1, cols + 1, tok, channels), BF16),
            vmem((2, 2) + q.shape, BF16),
            pltpu.SemaphoreType.DMA((3,)),
            vmem((8, n_q), F32),
            vmem((2, 8, n_q), F32),
            pltpu.SemaphoreType.DMA((2, 2)),
            vmem((per_key, n_q), F32),
            vmem((2, per_key, n_q), F32),
            vmem((slots, (cols + 1) * per_key, n_q), F32),
            vmem((slots, (cols + 1) * per_key, n_q), F32),
            vmem((slots, 8, n_q), F32),
            vmem((2, slots, per_key, n_q), F32),
            vmem((2, slots, per_key, n_q), F32),
            vmem((2, slots, 8, n_q), F32),
            vmem((2, chunks, HEADS_PER_CHUNK, cols, 4, per_col), F32),
            vmem((2, chunks, HEADS_PER_CHUNK, cols, 4, per_col), F32),
            vmem((2, grid_t, rows + 1, cols, tok, width), F32),
            vmem((2,) + q.shape, BF16),
            vmem((2,) + q.shape, BF16),
            vmem((2, grid_t, rows + 1, tok, channels), BF16),
            vmem((2, grid_t, rows, tok, channels), BF16),
            vmem((2, grid_t, tok, channels), BF16),
            vmem((2, grid_t, cols, tok, channels), BF16),
            vmem((2, grid_t, cols, tok, channels), BF16),
            vmem((3,) + q.shape, BF16),
            vmem((grid_t, rows, cols, tok, width), F32),
            vmem((2, grid_t, cols, tok, width), F32),
            pltpu.SemaphoreType.DMA((KINDS, chunks)),
            pltpu.SemaphoreType.DMA((KINDS, chunks)),
        ],
        compiler_params=pltpu.CompilerParams(
            collective_id=0, has_side_effects=True, vmem_limit_bytes=VMEM_KIB * 1024
        ),
    )(time_start.transpose(1, 2, 0), q, kv, go)
    return out[:, None]


def solution(mesh):
    sizes = (mesh.shape["section"], mesh.shape["ha"], mesh.shape["wa"])
    return jax.shard_map(
        functools.partial(local, sizes),
        mesh=mesh,
        in_specs=(
            P("section", None, "ha", "wa", None, None),
            P(None, "section", None, "ha", "wa", None, None),
            P("section", None, "ha", "wa", None, None),
            P(None, "ha", "wa"),
        ),
        out_specs=P(None, "section", None, "ha", "wa", None, None),
        check_vma=False,
    )
```

```python
import functools

import jax
import jax.numpy as jnp
from jax import lax
from jax.experimental import pallas as pl
from jax.experimental.pallas import tpu as pltpu
from jax.sharding import PartitionSpec as P

HEAD_DIM = 128
HEADS_PER_CHUNK = 1
MESH = pl.DeviceIdType.MESH
F32 = jnp.float32
BF16 = jnp.bfloat16

Y_KV, Z_Q, EXT, CORNER, STAT, DQ, EXT_INNER, EXT_EDGE, CORNER_PART, Y_PART, OUT, SHIFT, KINDS = (
    0, 1, 3, 4, 5, 7, 9, 10, 11, 12, 13, 14, 15)

AHEAD_Y = 6
AHEAD_Q = 3, 3
AHEAD_E = 3, 3
CORNERS_AHEAD = 2
STAT_LAG = 2
MERGE_LAG = 4
FOLD_LAG = 5
SHIFTED = 7
LOW = -1e30
VMEM_KIB = 56000


def dot(a, b, contract):
    return lax.dot_general(a, b, ((contract[0], contract[1]), ((), ())), preferred_element_type=F32)


def merge(top, lse, mean, lse_other, mean_other):
    most = jnp.maximum(lse, lse_other)
    w, w_other = jnp.exp(lse - most), jnp.exp(lse_other - most)
    inv = 1.0 / (w + w_other)
    return jnp.exp(top - most) * inv, (w * mean + w_other * mean_other) * inv


def kernel(sizes, starts, q_in, kv_in, go_in, out, qg, kx, qz, load_sem, first_send, first_recv, first_sem, bias,
           bias_z, e_own, dp_own, st_own, e_z, dp_z, st_z, stat_send, stat_recv, acc, dqz_send, dqz_recv,
           pz_send, pz_recv, pc_recv, py_send, py_recv, own, total_q, total_kv, send_sem, recv_sem):
    n_sec, n_ha, n_wa, chunks, width = sizes
    _, grid_t, rows, cols, tok, _ = qg.shape
    per_col = grid_t * rows * tok
    per_key = grid_t * (rows + 1) * tok
    slots = e_own.shape[0]
    sec, ha, wa = lax.axis_index("section"), lax.axis_index("ha"), lax.axis_index("wa")
    before = lax.rem(sec + n_sec - 1, n_sec)
    after = lax.rem(sec + 1, n_sec)
    other = 1 - ha
    edge = other * (rows - 1)
    inner = rows - 1 - edge
    has = (wa > 0, wa < n_wa - 1)
    peer = (wa - 1, wa + 1)
    near = (0, cols - 1)
    rim = (wa == 0) | (wa == n_wa - 1)
    by_rim = (wa == 1, wa == n_wa - 2)
    scale = HEAD_DIM ** (-0.5)

    staying = chunks - SHIFTED
    kept, moved_on = slice(0, staying * width), slice(staying * width, chunks * width)

    def held(at):
        return ((q_in, qg.at[0, :, :, :, :, at]), (go_in, qg.at[1, :, :, :, :, at]),
                (kv_in, kx.at[:, :, 0:rows, 0:cols, :, at]))

    loads = [pltpu.make_async_copy(src.at[(slice(None),) * (len(src.shape) - 1) + (kept,)], dst, load_sem.at[n])
             for n, (src, dst) in enumerate(held(kept))]
    for load in loads:
        load.start()

    n_q = cols * per_col
    lane = lax.broadcasted_iota(jnp.int32, (1, n_q), 1)
    first = jnp.zeros((1, n_q), F32)
    for c in range(cols):
        for t in range(grid_t):
            for r in range(rows):
                tile = (c * grid_t + t) * rows + r
                first = jnp.where(lane // tok == tile, starts[r, c, t].astype(F32), first)
    first_send[...] = jnp.broadcast_to(first, first_send.shape)

    barrier = pltpu.get_barrier_semaphore()

    def greet(*device):
        pl.semaphore_signal(barrier, inc=1, device_id=device, device_id_type=MESH)

    greet(before, ha, wa)
    greet(after, ha, wa)
    greet(sec, other, wa)
    for side in (0, 1):
        @pl.when(has[side])
        def _():
            greet(sec, ha, peer[side])

    sides_here = jnp.minimum(wa, 1) + jnp.minimum(n_wa - 1 - wa, 1)
    pl.semaphore_wait(barrier, 3 + sides_here)

    def keys_move(c):
        return (lax.rem(c, 3) == 2) & (c < chunks - 2)

    def lanes(c):
        return pl.ds(pl.multiple_of(c * width, width), width)

    def within(j):
        return slice(j * HEAD_DIM, (j + 1) * HEAD_DIM)

    def channels(c, j):
        return pl.ds(pl.multiple_of(c * width + j * HEAD_DIM, HEAD_DIM), HEAD_DIM)

    def remote(src, dst, sent, arrived, c, device):
        return pltpu.make_async_remote_copy(
            src_ref=src, dst_ref=dst, send_sem=send_sem.at[sent, c], recv_sem=recv_sem.at[arrived, c],
            device_id=device, device_id_type=MESH)

    shifts = [remote(src.at[(slice(None),) * (len(src.shape) - 1) + (moved_on,)], dst, SHIFT, SHIFT, n, (before, ha, wa))
              for n, (src, dst) in enumerate(held(moved_on))]

    def y_kv(c):
        return remote(kx.at[:, :, edge, 0:cols, :, lanes(c)], kx.at[:, :, rows, 0:cols, :, lanes(c)],
                      Y_KV, Y_KV, c, (sec, other, wa))

    def z_q(side, c, both):
        at = slice(0, cols) if both else slice(near[side], near[side] + 1)
        return remote(qg.at[:, :, :, at, :, lanes(c)], qz.at[1 - side, :, :, :, at, :, lanes(c)],
                      Z_Q + side, Z_Q + 1 - side, c, (sec, ha, peer[side]))

    def ext(side, c):
        return remote(kx.at[:, :, 0:rows, near[side], :, lanes(c)], kx.at[:, :, 0:rows, cols, :, lanes(c)],
                      EXT, EXT, c, (sec, ha, peer[side]))

    def corner(side, c):
        return remote(kx.at[:, :, rows, near[side], :, lanes(c)], kx.at[:, :, rows, cols, :, lanes(c)],
                      CORNER, CORNER, c, (sec, ha, peer[side]))

    def stat(side, c, both):
        at = slice(0, cols if both else 1)
        return remote(stat_send.at[side, c, :, at], stat_recv.at[1 - side, c, :, at],
                      STAT + side, STAT + 1 - side, c, (sec, ha, peer[side]))

    def dq_back(side, c, both):
        col = near[1 - side]
        at = slice(0, cols) if both else slice(col, col + 1)
        return remote(dqz_send.at[side, :, :, at, :, lanes(c)], dqz_recv.at[1 - side, :, :, at, :, lanes(c)],
                      DQ + side, DQ + 1 - side, c, (sec, ha, peer[side]))

    def ext_inner(side, c):
        return remote(pz_send.at[:, :, inner, :, lanes(c)], pz_recv.at[:, :, inner, :, lanes(c)],
                      EXT_INNER, EXT_INNER, c, (sec, ha, peer[side]))

    def ext_edge(side, c):
        return remote(pz_send.at[:, :, edge, :, lanes(c)], pz_recv.at[:, :, edge, :, lanes(c)],
                      EXT_EDGE, EXT_EDGE, c, (sec, ha, peer[side]))

    def corner_part(c):
        return remote(pz_send.at[:, :, rows, :, lanes(c)], pc_recv.at[:, :, :, lanes(c)],
                      CORNER_PART, CORNER_PART, c, (sec, other, wa))

    def y_part(c):
        return remote(py_send.at[:, :, :, :, lanes(c)], py_recv.at[:, :, :, :, lanes(c)],
                      Y_PART, Y_PART, c, (sec, other, wa))

    def result(*at):
        return remote(own.at[at], out.at[at], OUT, OUT, 0, (before, ha, wa))

    def kv_row(row, c):
        return pl.ds(1, 2), slice(None), row, slice(None), slice(None), lanes(c)

    def if_(cond, action):
        pl.when(cond)(action)

    def leaving(c, action):
        moved = keys_move(c)
        for side in (0, 1):
            if_(has[side] & rim & jnp.logical_not(moved), lambda: action(side, True))
            if_(has[side] & jnp.logical_not(rim), lambda: action(side, False))

    def coming(c, action):
        moved = keys_move(c)
        for side in (0, 1):
            if_(by_rim[side] & jnp.logical_not(moved), lambda: action(side, True))
            if_(has[side] & jnp.logical_not(by_rim[side]), lambda: action(side, False))

    def exchanged(c, action):
        moved = keys_move(c)
        for side in (0, 1):
            wide = (rim | by_rim[side]) & jnp.logical_not(moved)
            if_(has[side] & wide, lambda: action(side, True))
            if_(has[side] & jnp.logical_not(wide), lambda: action(side, False))

    def keys_leave(c, action):
        for side in (0, 1):
            if_(by_rim[side] & keys_move(c), lambda: action(side))

    def keys_come(c, action):
        for side in (0, 1):
            if_(has[side] & rim & keys_move(c), lambda: action(side))

    def queries_send(c):
        leaving(c, lambda side, both: z_q(side, c, both).start())

    def keys_send(c):
        keys_leave(c, lambda side: ext(side, c).start())

    def passes_corner(c):
        return (by_rim[0] | by_rim[1]) & keys_move(c)

    def stage_corner(c):
        if_(passes_corner(c), lambda: y_kv(c).wait_recv())
        keys_leave(c, lambda side: corner(side, c).start())

    def block(ref, lead, col, ch, n):
        return ref[lead + (slice(None), slice(None), col, slice(None), ch)].reshape(n, HEAD_DIM)

    def joined(ref, lead, at, ch, n):
        return jnp.concatenate([block(ref, lead, col, ch, n) for col in at])

    def first_phase(k, v, qh, gh, bias_of, e_ref, dp_ref, st_ref):
        s = dot(k, qh, ((1,), (1,))) * scale
        s = (s.reshape(-1, per_key, s.shape[1]) + bias_of).reshape(s.shape)
        top = jnp.max(s, axis=0, keepdims=True)
        e = jnp.exp(s - top)
        dp = dot(v, gh, ((1,), (1,)))
        total = jnp.sum(e, axis=0, keepdims=True)
        lse = top + jnp.log(total)
        mean = jnp.sum(e * dp, axis=0, keepdims=True) / total
        e_ref[...] = e
        dp_ref[...] = dp
        st_ref[0:1] = top
        st_ref[1:2] = lse
        st_ref[2:3] = mean
        return lse, mean

    def second_phase(k, qh, gh, e_ref, dp_ref, st_ref, lse_other, mean_other):
        factor, delta = merge(st_ref[0:1], st_ref[1:2], st_ref[2:3], lse_other, mean_other)
        p = e_ref[...] * factor
        ds = (p * (dp_ref[...] - delta)).astype(BF16)
        return (dot(ds, qh, ((1,), (0,))) * scale, dot(p.astype(BF16), gh, ((1,), (0,))),
                dot(ds, k, ((0,), (0,))) * scale)

    def own_first(key_cols, c, j):
        ch, b = channels(c, j), lax.rem(c, slots // HEADS_PER_CHUNK) * HEADS_PER_CHUNK + j
        n = key_cols * per_key
        lse, mean = first_phase(
            joined(kx, (0,), range(key_cols), ch, per_key), joined(kx, (1,), range(key_cols), ch, per_key),
            joined(qg, (0,), range(cols), ch, per_col), joined(qg, (1,), range(cols), ch, per_col),
            bias[...], e_own.at[b, 0:n], dp_own.at[b, 0:n], st_own.at[b])
        for row, value in enumerate((lse, mean)):
            for side, order in ((0, (0, 1)), (1, (1, 0))):
                for n, col in enumerate(order):
                    stat_send[side, c, j, n, row:row + 1] = value[:, col * per_col:(col + 1) * per_col]

    def own_second(key_cols, c, j):
        ch, b = channels(c, j), lax.rem(c, slots // HEADS_PER_CHUNK) * HEADS_PER_CHUNK + j
        n = key_cols * per_key
        if key_cols > cols:
            lse_other, mean_other = LOW, 0.0
        else:
            def pick(row):
                at = slice(row, row + 1)
                low = jnp.where(has[0], stat_recv[0, c, j, 0, at], stat_recv[1, c, j, 1, at])
                high = jnp.where(has[1], stat_recv[1, c, j, 0, at], stat_recv[0, c, j, 1, at])
                return jnp.concatenate([low, high], axis=1)

            lse_other, mean_other = pick(2), pick(3)
        dk, dv, dqh = second_phase(
            joined(kx, (0,), range(key_cols), ch, per_key),
            joined(qg, (0,), range(cols), ch, per_col), joined(qg, (1,), range(cols), ch, per_col),
            e_own.at[b, 0:n], dp_own.at[b, 0:n], st_own.at[b], lse_other, mean_other)
        for i, grad in enumerate((dk, dv)):
            for col in range(key_cols):
                part = grad[col * per_key:(col + 1) * per_key].reshape(grid_t, rows + 1, tok, HEAD_DIM)
                if col < cols:
                    acc[i, :, :, col, :, within(j)] = part
                else:
                    pz_send[i, :, :, :, ch] = part.astype(BF16)
        for col in range(cols):
            part = dqh[col * per_col:(col + 1) * per_col].astype(BF16)
            own[0, :, :, col, :, ch] = part.reshape(grid_t, rows, tok, HEAD_DIM)

    def columns(side, both):
        return (near[1 - side], near[side]) if both else (near[1 - side],)

    def z_first(side, both, c, j):
        ch, b = channels(c, j), lax.rem(c, slots // HEADS_PER_CHUNK) * HEADS_PER_CHUNK + j
        at = columns(side, both)
        n = len(at) * per_col
        lse, mean = first_phase(
            block(kx, (0,), near[side], ch, per_key), block(kx, (1,), near[side], ch, per_key),
            joined(qz, (side, 0), at, ch, per_col), joined(qz, (side, 1), at, ch, per_col),
            bias_z[side, :, 0:n], e_z.at[side, b, :, 0:n], dp_z.at[side, b, :, 0:n], st_z.at[side, b, :, 0:n])
        for row, value in ((2, lse), (3, mean)):
            for m in range(len(at)):
                stat_send[side, c, j, m, row:row + 1] = value[:, m * per_col:(m + 1) * per_col]

    def z_second(side, both, c, j):
        ch, b = channels(c, j), lax.rem(c, slots // HEADS_PER_CHUNK) * HEADS_PER_CHUNK + j
        at = columns(side, both)
        n = len(at) * per_col
        dk, dv, dqh = second_phase(
            block(kx, (0,), near[side], ch, per_key),
            joined(qz, (side, 0), at, ch, per_col), joined(qz, (side, 1), at, ch, per_col),
            e_z.at[side, b, :, 0:n], dp_z.at[side, b, :, 0:n], st_z.at[side, b, :, 0:n],
            *(jnp.concatenate([stat_recv[side, c, j, m, row:row + 1] for m in range(len(at))], axis=1)
              for row in (0, 1)))
        for i, grad in enumerate((dk, dv)):
            acc[i, :, :, near[side], :, within(j)] += grad.reshape(grid_t, rows + 1, tok, HEAD_DIM)
        for m, col in enumerate(at):
            part = dqh[m * per_col:(m + 1) * per_col].astype(BF16)
            dqz_send[side, :, :, col, :, ch] = part.reshape(grid_t, rows, tok, HEAD_DIM)

    def heads(action):
        for j in range(HEADS_PER_CHUNK):
            action(j)

    def stage_first(c):
        if_(jnp.logical_not(passes_corner(c)), lambda: y_kv(c).wait_recv())

        def arrive(side):
            ext(1 - side, c).wait_recv()
            corner(1 - side, c).wait_recv()

        keys_come(c, arrive)
        far = rim & keys_move(c)
        if_(far, lambda: heads(lambda j: own_first(cols + 1, c, j)))
        if_(jnp.logical_not(far), lambda: heads(lambda j: own_first(cols, c, j)))

        def from_side(side, both):
            z_q(1 - side, c, both).wait_recv()
            heads(lambda j: z_first(side, both, c, j))

        coming(c, from_side)
        exchanged(c, lambda side, both: stat(side, c, both).start())

    def stage_second(c):
        exchanged(c, lambda side, both: stat(1 - side, c, both).wait_recv())
        far = rim & keys_move(c)
        if_(far, lambda: heads(lambda j: own_second(cols + 1, c, j)))
        if_(jnp.logical_not(far), lambda: heads(lambda j: own_second(cols, c, j)))

        def extra(side):
            ext_inner(side, c).start()
            corner_part(c).start()

        keys_come(c, extra)

        def from_side(side, both):
            heads(lambda j: z_second(side, both, c, j))
            dq_back(side, c, both).start()

        coming(c, from_side)
        ch = lanes(c)
        py_send[:, :, :, :, ch] = acc[:, :, rows].astype(BF16)
        y_part(c).start()
        own[1:3, :, :, :, :, ch] = acc[:, :, 0:rows].astype(BF16)
        if_(jnp.logical_not(passes_corner(c)) & (c < staying), lambda: result(*kv_row(inner, c)).start())

    def sent(c):
        y_kv(c).wait_send()
        leaving(c, lambda side, both: z_q(side, c, both).wait_send())

        def keys_sent(side):
            ext(side, c).wait_send()
            corner(side, c).wait_send()

        keys_leave(c, keys_sent)

        def extra_sent(side):
            ext_inner(side, c).wait_send()
            ext_edge(side, c).wait_send()
            corner_part(c).wait_send()

        keys_come(c, extra_sent)
        exchanged(c, lambda side, both: stat(side, c, both).wait_send())
        coming(c, lambda side, both: dq_back(side, c, both).wait_send())
        y_part(c).wait_send()

    def stage_merge(c):
        ch = lanes(c)

        def merged(side):
            corner_part(c).wait_recv()
            pz_send[:, :, edge, :, ch] = (
                pz_send[:, :, edge, :, ch].astype(F32) + pc_recv[:, :, :, ch].astype(F32)).astype(BF16)
            ext_edge(side, c).start()

        keys_come(c, merged)

    def stage_fold(c):
        ch = lanes(c)
        y_part(c).wait_recv()
        total_kv[...] = own[1:3, :, edge, :, :, ch].astype(F32) + py_recv[:, :, :, :, ch].astype(F32)

        def fold(side):
            ext_edge(1 - side, c).wait_recv()
            total_kv[:, :, near[side]] += pz_recv[:, :, edge, :, ch].astype(F32)
            ext_inner(1 - side, c).wait_recv()
            own[1:3, :, inner, near[side], :, ch] = (
                own[1:3, :, inner, near[side], :, ch].astype(F32) + pz_recv[:, :, inner, :, ch].astype(F32)).astype(BF16)
            if_(c < staying, lambda: result(*kv_row(inner, c)).start())

        keys_leave(c, fold)
        own[1:3, :, edge, :, :, ch] = total_kv[...].astype(BF16)
        if_(c < staying, lambda: result(*kv_row(edge, c)).start())
        total_q[...] = own[0, :, :, :, :, ch].astype(F32)

        def back(side, both):
            dq_back(1 - side, c, both).wait_recv()
            for col in (range(cols) if both else (near[side],)):
                total_q[:, :, col] += dqz_recv[side, :, :, col, :, ch].astype(F32)

        leaving(c, back)

        def leave():
            own[0, :, :, :, :, ch] = total_q[...].astype(BF16)
            result(0, slice(None), slice(None), slice(None), slice(None), ch).start()

        def stay():
            out[0, :, :, :, :, ch] = total_q[...].astype(BF16)
            out[1:3, :, :, :, :, ch] = own[1:3, :, :, :, :, ch]

        if_(c < staying, leave)
        if_(c >= staying, stay)
        sent(c)

    def first_copy(side):
        return pltpu.make_async_remote_copy(
            src_ref=first_send, dst_ref=first_recv.at[1 - side], send_sem=first_sem.at[0, side],
            recv_sem=first_sem.at[1, 1 - side], device_id=(sec, ha, peer[side]), device_id_type=MESH)

    for side in (0, 1):
        if_(has[side], lambda: first_copy(side).start())

    for shift in shifts:
        shift.start()
    for load in loads:
        load.wait()
    ahead_q, ahead_e = (jnp.where(lax.rem(sec, 2) == 0, a, b) for a, b in (AHEAD_Q, AHEAD_E))
    for c in range(max(AHEAD_Y, *AHEAD_Q, *AHEAD_E)):
        if c < AHEAD_Y:
            y_kv(c).start()
        if_(c < ahead_q, lambda: queries_send(c))
        if_(c < ahead_e, lambda: keys_send(c))

    def window(ref, begin):
        per_t = (rows + 1) * tok
        for t in range(grid_t):
            seen = (begin <= t) & (begin + 2 >= t)
            row = jnp.where(seen, 0.0, LOW).astype(F32)
            ref[t * per_t:(t + 1) * per_t, :] = jnp.broadcast_to(row, (per_t, n_q))

    window(bias, first)
    for c in range(CORNERS_AHEAD):
        stage_corner(c)
    for side in (0, 1):
        def _(side=side):
            first_copy(1 - side).wait_recv()
            begin = jnp.concatenate(
                [first_recv[side, 0:1, col * per_col:(col + 1) * per_col] for col in columns(side, True)], axis=1)
            window(bias_z.at[side], begin)
        if_(has[side], _)

    def step(i, carry):
        def arrived():
            for shift in shifts:
                shift.wait_recv()

        if_(i + AHEAD_Y == staying, arrived)
        if_(i + AHEAD_Y < chunks, lambda: y_kv(i + AHEAD_Y).start())
        if_(i + ahead_q < chunks, lambda: queries_send(i + ahead_q))
        if_(i + ahead_e < chunks, lambda: keys_send(i + ahead_e))
        if_(i + CORNERS_AHEAD < chunks, lambda: stage_corner(i + CORNERS_AHEAD))
        if_(i < chunks, lambda: stage_first(i))
        if_((i >= MERGE_LAG) & (i < chunks + MERGE_LAG), lambda: stage_merge(i - MERGE_LAG))
        if_((i >= STAT_LAG) & (i < chunks + STAT_LAG), lambda: stage_second(i - STAT_LAG))
        if_(i >= FOLD_LAG, lambda: stage_fold(i - FOLD_LAG))
        return carry

    lax.fori_loop(0, chunks + FOLD_LAG, step, 0)
    result(slice(None), slice(None), slice(None), slice(None), slice(None), kept).wait()
    for shift in shifts:
        shift.wait_send()
    for side in (0, 1):
        if_(has[side], lambda: first_copy(side).wait_send())


def local(mesh_sizes, queries, keys_values, grad_out, time_start):
    n_sec, n_ha, n_wa = mesh_sizes
    q, kv, go = queries[0], keys_values[:, 0], grad_out[0]
    grid_t, rows, cols, tok, channels = q.shape
    assert n_ha == 2 and rows == 2 and cols == 2 and n_wa >= 4 and n_sec >= 2
    width = HEADS_PER_CHUNK * HEAD_DIM
    assert channels % width == 0
    chunks = channels // width
    assert chunks >= max(AHEAD_Y, *AHEAD_Q, *AHEAD_E) and AHEAD_Y >= CORNERS_AHEAD
    assert AHEAD_Y >= max(*AHEAD_Q, *AHEAD_E) and chunks - SHIFTED >= AHEAD_Y and SHIFTED > 0
    per_col, per_key = grid_t * rows * tok, grid_t * (rows + 1) * tok
    n_q = cols * per_col
    slots = (STAT_LAG + 1) * HEADS_PER_CHUNK
    stay = pl.BlockSpec(memory_space=pl.ANY)
    vmem = pltpu.VMEM
    out = pl.pallas_call(
        functools.partial(kernel, (n_sec, n_ha, n_wa, chunks, width)),
        out_shape=pltpu.VMEM((3,) + q.shape, BF16),
        in_specs=[pl.BlockSpec(memory_space=pltpu.SMEM), stay, stay, stay],
        out_specs=pl.BlockSpec(memory_space=pltpu.VMEM),
        scratch_shapes=[
            vmem((2,) + q.shape, BF16),
            vmem((2, grid_t, rows + 1, cols + 1, tok, channels), BF16),
            vmem((2, 2) + q.shape, BF16),
            pltpu.SemaphoreType.DMA((3,)),
            vmem((8, n_q), F32),
            vmem((2, 8, n_q), F32),
            pltpu.SemaphoreType.DMA((2, 2)),
            vmem((per_key, n_q), F32),
            vmem((2, per_key, n_q), F32),
            vmem((slots, (cols + 1) * per_key, n_q), F32),
            vmem((slots, (cols + 1) * per_key, n_q), F32),
            vmem((slots, 8, n_q), F32),
            vmem((2, slots, per_key, n_q), F32),
            vmem((2, slots, per_key, n_q), F32),
            vmem((2, slots, 8, n_q), F32),
            vmem((2, chunks, HEADS_PER_CHUNK, cols, 4, per_col), F32),
            vmem((2, chunks, HEADS_PER_CHUNK, cols, 4, per_col), F32),
            vmem((2, grid_t, rows + 1, cols, tok, width), F32),
            vmem((2,) + q.shape, BF16),
            vmem((2,) + q.shape, BF16),
            vmem((2, grid_t, rows + 1, tok, channels), BF16),
            vmem((2, grid_t, rows, tok, channels), BF16),
            vmem((2, grid_t, tok, channels), BF16),
            vmem((2, grid_t, cols, tok, channels), BF16),
            vmem((2, grid_t, cols, tok, channels), BF16),
            vmem((3,) + q.shape, BF16),
            vmem((grid_t, rows, cols, tok, width), F32),
            vmem((2, grid_t, cols, tok, width), F32),
            pltpu.SemaphoreType.DMA((KINDS, chunks)),
            pltpu.SemaphoreType.DMA((KINDS, chunks)),
        ],
        compiler_params=pltpu.CompilerParams(
            collective_id=0, has_side_effects=True, vmem_limit_bytes=VMEM_KIB * 1024
        ),
    )(time_start.transpose(1, 2, 0), q, kv, go)
    return out[:, None]


def solution(mesh):
    sizes = (mesh.shape["section"], mesh.shape["ha"], mesh.shape["wa"])
    return jax.shard_map(
        functools.partial(local, sizes),
        mesh=mesh,
        in_specs=(
            P("section", None, "ha", "wa", None, None),
            P(None, "section", None, "ha", "wa", None, None),
            P("section", None, "ha", "wa", None, None),
            P(None, "ha", "wa"),
        ),
        out_specs=P(None, "section", None, "ha", "wa", None, None),
        check_vma=False,
    )
```

```python
import functools

import jax
import jax.numpy as jnp
from jax import lax
from jax.experimental import pallas as pl
from jax.experimental.pallas import tpu as pltpu
from jax.sharding import PartitionSpec as P

HEAD_DIM = 128
HEADS_PER_CHUNK = 1
MESH = pl.DeviceIdType.MESH
F32 = jnp.float32
BF16 = jnp.bfloat16

Y_KV, Z_Q, EXT, CORNER, STAT, DQ, EXT_INNER, EXT_EDGE, CORNER_PART, Y_PART, OUT, SHIFT, KINDS = (
    0, 1, 3, 4, 5, 7, 9, 10, 11, 12, 13, 14, 15)

AHEAD_Y = 5
AHEAD_Q = 3, 3
AHEAD_E = 3, 3
CORNERS_AHEAD = 2
STAT_LAG = 2
MERGE_LAG = 4
FOLD_LAG = 5
SHIFTED = 7
LOW = -1e30
VMEM_KIB = 56000


def dot(a, b, contract):
    return lax.dot_general(a, b, ((contract[0], contract[1]), ((), ())), preferred_element_type=F32)


def merge(top, lse, mean, lse_other, mean_other):
    most = jnp.maximum(lse, lse_other)
    w, w_other = jnp.exp(lse - most), jnp.exp(lse_other - most)
    inv = 1.0 / (w + w_other)
    return jnp.exp(top - most) * inv, (w * mean + w_other * mean_other) * inv


def kernel(sizes, starts, q_in, kv_in, go_in, out, qg, kx, qz, load_sem, first_send, first_recv, first_sem, bias,
           bias_z, e_own, dp_own, st_own, e_z, dp_z, st_z, stat_send, stat_recv, acc, dqz_send, dqz_recv,
           pz_send, pz_recv, pc_recv, py_send, py_recv, own, total_q, total_kv, send_sem, recv_sem):
    n_sec, n_ha, n_wa, chunks, width = sizes
    _, grid_t, rows, cols, tok, _ = qg.shape
    per_col = grid_t * rows * tok
    per_key = grid_t * (rows + 1) * tok
    slots = e_own.shape[0]
    sec, ha, wa = lax.axis_index("section"), lax.axis_index("ha"), lax.axis_index("wa")
    before = lax.rem(sec + n_sec - 1, n_sec)
    after = lax.rem(sec + 1, n_sec)
    other = 1 - ha
    edge = other * (rows - 1)
    inner = rows - 1 - edge
    has = (wa > 0, wa < n_wa - 1)
    peer = (wa - 1, wa + 1)
    near = (0, cols - 1)
    rim = (wa == 0) | (wa == n_wa - 1)
    by_rim = (wa == 1, wa == n_wa - 2)
    scale = HEAD_DIM ** (-0.5)

    staying = chunks - SHIFTED
    kept, moved_on = slice(0, staying * width), slice(staying * width, chunks * width)

    def held(at):
        return ((q_in, qg.at[0, :, :, :, :, at]), (go_in, qg.at[1, :, :, :, :, at]),
                (kv_in, kx.at[:, :, 0:rows, 0:cols, :, at]))

    loads = [pltpu.make_async_copy(src.at[(slice(None),) * (len(src.shape) - 1) + (kept,)], dst, load_sem.at[n])
             for n, (src, dst) in enumerate(held(kept))]
    for load in loads:
        load.start()

    n_q = cols * per_col
    lane = lax.broadcasted_iota(jnp.int32, (1, n_q), 1)
    first = jnp.zeros((1, n_q), F32)
    for c in range(cols):
        for t in range(grid_t):
            for r in range(rows):
                tile = (c * grid_t + t) * rows + r
                first = jnp.where(lane // tok == tile, starts[r, c, t].astype(F32), first)
    first_send[...] = jnp.broadcast_to(first, first_send.shape)

    barrier = pltpu.get_barrier_semaphore()

    def greet(*device):
        pl.semaphore_signal(barrier, inc=1, device_id=device, device_id_type=MESH)

    greet(before, ha, wa)
    greet(after, ha, wa)
    greet(sec, other, wa)
    for side in (0, 1):
        @pl.when(has[side])
        def _():
            greet(sec, ha, peer[side])

    sides_here = jnp.minimum(wa, 1) + jnp.minimum(n_wa - 1 - wa, 1)
    pl.semaphore_wait(barrier, 3 + sides_here)

    def keys_move(c):
        return (lax.rem(c, 3) == 2) & (c < chunks - 2)

    def lanes(c):
        return pl.ds(pl.multiple_of(c * width, width), width)

    def within(j):
        return slice(j * HEAD_DIM, (j + 1) * HEAD_DIM)

    def channels(c, j):
        return pl.ds(pl.multiple_of(c * width + j * HEAD_DIM, HEAD_DIM), HEAD_DIM)

    def remote(src, dst, sent, arrived, c, device):
        return pltpu.make_async_remote_copy(
            src_ref=src, dst_ref=dst, send_sem=send_sem.at[sent, c], recv_sem=recv_sem.at[arrived, c],
            device_id=device, device_id_type=MESH)

    shifts = [remote(src.at[(slice(None),) * (len(src.shape) - 1) + (moved_on,)], dst, SHIFT, SHIFT, n, (before, ha, wa))
              for n, (src, dst) in enumerate(held(moved_on))]

    def y_kv(c):
        return remote(kx.at[:, :, edge, 0:cols, :, lanes(c)], kx.at[:, :, rows, 0:cols, :, lanes(c)],
                      Y_KV, Y_KV, c, (sec, other, wa))

    def z_q(side, c, both):
        at = slice(0, cols) if both else slice(near[side], near[side] + 1)
        return remote(qg.at[:, :, :, at, :, lanes(c)], qz.at[1 - side, :, :, :, at, :, lanes(c)],
                      Z_Q + side, Z_Q + 1 - side, c, (sec, ha, peer[side]))

    def ext(side, c):
        return remote(kx.at[:, :, 0:rows, near[side], :, lanes(c)], kx.at[:, :, 0:rows, cols, :, lanes(c)],
                      EXT, EXT, c, (sec, ha, peer[side]))

    def corner(side, c):
        return remote(kx.at[:, :, rows, near[side], :, lanes(c)], kx.at[:, :, rows, cols, :, lanes(c)],
                      CORNER, CORNER, c, (sec, ha, peer[side]))

    def stat(side, c, both):
        at = slice(0, cols if both else 1)
        return remote(stat_send.at[side, c, :, at], stat_recv.at[1 - side, c, :, at],
                      STAT + side, STAT + 1 - side, c, (sec, ha, peer[side]))

    def dq_back(side, c, both):
        col = near[1 - side]
        at = slice(0, cols) if both else slice(col, col + 1)
        return remote(dqz_send.at[side, :, :, at, :, lanes(c)], dqz_recv.at[1 - side, :, :, at, :, lanes(c)],
                      DQ + side, DQ + 1 - side, c, (sec, ha, peer[side]))

    def ext_inner(side, c):
        return remote(pz_send.at[:, :, inner, :, lanes(c)], pz_recv.at[:, :, inner, :, lanes(c)],
                      EXT_INNER, EXT_INNER, c, (sec, ha, peer[side]))

    def ext_edge(side, c):
        return remote(pz_send.at[:, :, edge, :, lanes(c)], pz_recv.at[:, :, edge, :, lanes(c)],
                      EXT_EDGE, EXT_EDGE, c, (sec, ha, peer[side]))

    def corner_part(c):
        return remote(pz_send.at[:, :, rows, :, lanes(c)], pc_recv.at[:, :, :, lanes(c)],
                      CORNER_PART, CORNER_PART, c, (sec, other, wa))

    def y_part(c):
        return remote(py_send.at[:, :, :, :, lanes(c)], py_recv.at[:, :, :, :, lanes(c)],
                      Y_PART, Y_PART, c, (sec, other, wa))

    def result(*at):
        return remote(own.at[at], out.at[at], OUT, OUT, 0, (before, ha, wa))

    def kv_row(row, c):
        return pl.ds(1, 2), slice(None), row, slice(None), slice(None), lanes(c)

    def if_(cond, action):
        pl.when(cond)(action)

    def leaving(c, action):
        moved = keys_move(c)
        for side in (0, 1):
            if_(has[side] & rim & jnp.logical_not(moved), lambda: action(side, True))
            if_(has[side] & jnp.logical_not(rim), lambda: action(side, False))

    def coming(c, action):
        moved = keys_move(c)
        for side in (0, 1):
            if_(by_rim[side] & jnp.logical_not(moved), lambda: action(side, True))
            if_(has[side] & jnp.logical_not(by_rim[side]), lambda: action(side, False))

    def exchanged(c, action):
        moved = keys_move(c)
        for side in (0, 1):
            wide = (rim | by_rim[side]) & jnp.logical_not(moved)
            if_(has[side] & wide, lambda: action(side, True))
            if_(has[side] & jnp.logical_not(wide), lambda: action(side, False))

    def keys_leave(c, action):
        for side in (0, 1):
            if_(by_rim[side] & keys_move(c), lambda: action(side))

    def keys_come(c, action):
        for side in (0, 1):
            if_(has[side] & rim & keys_move(c), lambda: action(side))

    def queries_send(c):
        leaving(c, lambda side, both: z_q(side, c, both).start())

    def keys_send(c):
        keys_leave(c, lambda side: ext(side, c).start())

    def passes_corner(c):
        return (by_rim[0] | by_rim[1]) & keys_move(c)

    def stage_corner(c):
        if_(passes_corner(c), lambda: y_kv(c).wait_recv())
        keys_leave(c, lambda side: corner(side, c).start())

    def block(ref, lead, col, ch, n):
        return ref[lead + (slice(None), slice(None), col, slice(None), ch)].reshape(n, HEAD_DIM)

    def joined(ref, lead, at, ch, n):
        return jnp.concatenate([block(ref, lead, col, ch, n) for col in at])

    def first_phase(k, v, qh, gh, bias_of, e_ref, dp_ref, st_ref):
        s = dot(k, qh, ((1,), (1,))) * scale
        s = (s.reshape(-1, per_key, s.shape[1]) + bias_of).reshape(s.shape)
        top = jnp.max(s, axis=0, keepdims=True)
        e = jnp.exp(s - top)
        dp = dot(v, gh, ((1,), (1,)))
        total = jnp.sum(e, axis=0, keepdims=True)
        lse = top + jnp.log(total)
        mean = jnp.sum(e * dp, axis=0, keepdims=True) / total
        e_ref[...] = e
        dp_ref[...] = dp
        st_ref[0:1] = top
        st_ref[1:2] = lse
        st_ref[2:3] = mean
        return lse, mean

    def second_phase(k, qh, gh, e_ref, dp_ref, st_ref, lse_other, mean_other):
        factor, delta = merge(st_ref[0:1], st_ref[1:2], st_ref[2:3], lse_other, mean_other)
        p = e_ref[...] * factor
        ds = (p * (dp_ref[...] - delta)).astype(BF16)
        return (dot(ds, qh, ((1,), (0,))) * scale, dot(p.astype(BF16), gh, ((1,), (0,))),
                dot(ds, k, ((0,), (0,))) * scale)

    def own_first(key_cols, c, j):
        ch, b = channels(c, j), lax.rem(c, slots // HEADS_PER_CHUNK) * HEADS_PER_CHUNK + j
        n = key_cols * per_key
        lse, mean = first_phase(
            joined(kx, (0,), range(key_cols), ch, per_key), joined(kx, (1,), range(key_cols), ch, per_key),
            joined(qg, (0,), range(cols), ch, per_col), joined(qg, (1,), range(cols), ch, per_col),
            bias[...], e_own.at[b, 0:n], dp_own.at[b, 0:n], st_own.at[b])
        for row, value in enumerate((lse, mean)):
            for side, order in ((0, (0, 1)), (1, (1, 0))):
                for n, col in enumerate(order):
                    stat_send[side, c, j, n, row:row + 1] = value[:, col * per_col:(col + 1) * per_col]

    def own_second(key_cols, c, j):
        ch, b = channels(c, j), lax.rem(c, slots // HEADS_PER_CHUNK) * HEADS_PER_CHUNK + j
        n = key_cols * per_key
        if key_cols > cols:
            lse_other, mean_other = LOW, 0.0
        else:
            def pick(row):
                at = slice(row, row + 1)
                low = jnp.where(has[0], stat_recv[0, c, j, 0, at], stat_recv[1, c, j, 1, at])
                high = jnp.where(has[1], stat_recv[1, c, j, 0, at], stat_recv[0, c, j, 1, at])
                return jnp.concatenate([low, high], axis=1)

            lse_other, mean_other = pick(2), pick(3)
        dk, dv, dqh = second_phase(
            joined(kx, (0,), range(key_cols), ch, per_key),
            joined(qg, (0,), range(cols), ch, per_col), joined(qg, (1,), range(cols), ch, per_col),
            e_own.at[b, 0:n], dp_own.at[b, 0:n], st_own.at[b], lse_other, mean_other)
        for i, grad in enumerate((dk, dv)):
            for col in range(key_cols):
                part = grad[col * per_key:(col + 1) * per_key].reshape(grid_t, rows + 1, tok, HEAD_DIM)
                if col < cols:
                    acc[i, :, :, col, :, within(j)] = part
                else:
                    pz_send[i, :, :, :, ch] = part.astype(BF16)
        for col in range(cols):
            part = dqh[col * per_col:(col + 1) * per_col].astype(BF16)
            own[0, :, :, col, :, ch] = part.reshape(grid_t, rows, tok, HEAD_DIM)

    def columns(side, both):
        return (near[1 - side], near[side]) if both else (near[1 - side],)

    def z_first(side, both, c, j):
        ch, b = channels(c, j), lax.rem(c, slots // HEADS_PER_CHUNK) * HEADS_PER_CHUNK + j
        at = columns(side, both)
        n = len(at) * per_col
        lse, mean = first_phase(
            block(kx, (0,), near[side], ch, per_key), block(kx, (1,), near[side], ch, per_key),
            joined(qz, (side, 0), at, ch, per_col), joined(qz, (side, 1), at, ch, per_col),
            bias_z[side, :, 0:n], e_z.at[side, b, :, 0:n], dp_z.at[side, b, :, 0:n], st_z.at[side, b, :, 0:n])
        for row, value in ((2, lse), (3, mean)):
            for m in range(len(at)):
                stat_send[side, c, j, m, row:row + 1] = value[:, m * per_col:(m + 1) * per_col]

    def z_second(side, both, c, j):
        ch, b = channels(c, j), lax.rem(c, slots // HEADS_PER_CHUNK) * HEADS_PER_CHUNK + j
        at = columns(side, both)
        n = len(at) * per_col
        dk, dv, dqh = second_phase(
            block(kx, (0,), near[side], ch, per_key),
            joined(qz, (side, 0), at, ch, per_col), joined(qz, (side, 1), at, ch, per_col),
            e_z.at[side, b, :, 0:n], dp_z.at[side, b, :, 0:n], st_z.at[side, b, :, 0:n],
            *(jnp.concatenate([stat_recv[side, c, j, m, row:row + 1] for m in range(len(at))], axis=1)
              for row in (0, 1)))
        for i, grad in enumerate((dk, dv)):
            acc[i, :, :, near[side], :, within(j)] += grad.reshape(grid_t, rows + 1, tok, HEAD_DIM)
        for m, col in enumerate(at):
            part = dqh[m * per_col:(m + 1) * per_col].astype(BF16)
            dqz_send[side, :, :, col, :, ch] = part.reshape(grid_t, rows, tok, HEAD_DIM)

    def heads(action):
        for j in range(HEADS_PER_CHUNK):
            action(j)

    def stage_first(c):
        if_(jnp.logical_not(passes_corner(c)), lambda: y_kv(c).wait_recv())

        def arrive(side):
            ext(1 - side, c).wait_recv()
            corner(1 - side, c).wait_recv()

        keys_come(c, arrive)
        far = rim & keys_move(c)
        if_(far, lambda: heads(lambda j: own_first(cols + 1, c, j)))
        if_(jnp.logical_not(far), lambda: heads(lambda j: own_first(cols, c, j)))

        def from_side(side, both):
            z_q(1 - side, c, both).wait_recv()
            heads(lambda j: z_first(side, both, c, j))

        coming(c, from_side)
        exchanged(c, lambda side, both: stat(side, c, both).start())

    def stage_second(c):
        exchanged(c, lambda side, both: stat(1 - side, c, both).wait_recv())
        far = rim & keys_move(c)
        if_(far, lambda: heads(lambda j: own_second(cols + 1, c, j)))
        if_(jnp.logical_not(far), lambda: heads(lambda j: own_second(cols, c, j)))

        def extra(side):
            ext_inner(side, c).start()
            corner_part(c).start()

        keys_come(c, extra)

        def from_side(side, both):
            heads(lambda j: z_second(side, both, c, j))
            dq_back(side, c, both).start()

        coming(c, from_side)
        ch = lanes(c)
        py_send[:, :, :, :, ch] = acc[:, :, rows].astype(BF16)
        y_part(c).start()
        own[1:3, :, :, :, :, ch] = acc[:, :, 0:rows].astype(BF16)
        if_(jnp.logical_not(passes_corner(c)) & (c < staying), lambda: result(*kv_row(inner, c)).start())

    def sent(c):
        y_kv(c).wait_send()
        leaving(c, lambda side, both: z_q(side, c, both).wait_send())

        def keys_sent(side):
            ext(side, c).wait_send()
            corner(side, c).wait_send()

        keys_leave(c, keys_sent)

        def extra_sent(side):
            ext_inner(side, c).wait_send()
            ext_edge(side, c).wait_send()
            corner_part(c).wait_send()

        keys_come(c, extra_sent)
        exchanged(c, lambda side, both: stat(side, c, both).wait_send())
        coming(c, lambda side, both: dq_back(side, c, both).wait_send())
        y_part(c).wait_send()

    def stage_merge(c):
        ch = lanes(c)

        def merged(side):
            corner_part(c).wait_recv()
            pz_send[:, :, edge, :, ch] = (
                pz_send[:, :, edge, :, ch].astype(F32) + pc_recv[:, :, :, ch].astype(F32)).astype(BF16)
            ext_edge(side, c).start()

        keys_come(c, merged)

    def stage_fold(c):
        ch = lanes(c)
        y_part(c).wait_recv()
        total_kv[...] = own[1:3, :, edge, :, :, ch].astype(F32) + py_recv[:, :, :, :, ch].astype(F32)

        def fold(side):
            ext_edge(1 - side, c).wait_recv()
            total_kv[:, :, near[side]] += pz_recv[:, :, edge, :, ch].astype(F32)
            ext_inner(1 - side, c).wait_recv()
            own[1:3, :, inner, near[side], :, ch] = (
                own[1:3, :, inner, near[side], :, ch].astype(F32) + pz_recv[:, :, inner, :, ch].astype(F32)).astype(BF16)
            if_(c < staying, lambda: result(*kv_row(inner, c)).start())

        keys_leave(c, fold)
        own[1:3, :, edge, :, :, ch] = total_kv[...].astype(BF16)
        if_(c < staying, lambda: result(*kv_row(edge, c)).start())
        total_q[...] = own[0, :, :, :, :, ch].astype(F32)

        def back(side, both):
            dq_back(1 - side, c, both).wait_recv()
            for col in (range(cols) if both else (near[side],)):
                total_q[:, :, col] += dqz_recv[side, :, :, col, :, ch].astype(F32)

        leaving(c, back)

        def leave():
            own[0, :, :, :, :, ch] = total_q[...].astype(BF16)
            result(0, slice(None), slice(None), slice(None), slice(None), ch).start()

        def stay():
            out[0, :, :, :, :, ch] = total_q[...].astype(BF16)
            out[1:3, :, :, :, :, ch] = own[1:3, :, :, :, :, ch]

        if_(c < staying, leave)
        if_(c >= staying, stay)
        sent(c)

    def first_copy(side):
        return pltpu.make_async_remote_copy(
            src_ref=first_send, dst_ref=first_recv.at[1 - side], send_sem=first_sem.at[0, side],
            recv_sem=first_sem.at[1, 1 - side], device_id=(sec, ha, peer[side]), device_id_type=MESH)

    for side in (0, 1):
        if_(has[side], lambda: first_copy(side).start())

    for load in loads:
        load.wait()
    ahead_q, ahead_e = (jnp.where(lax.rem(sec, 2) == 0, a, b) for a, b in (AHEAD_Q, AHEAD_E))
    for c in range(max(AHEAD_Y, *AHEAD_Q, *AHEAD_E)):
        if c < AHEAD_Y:
            y_kv(c).start()
        if_(c < ahead_q, lambda: queries_send(c))
        if_(c < ahead_e, lambda: keys_send(c))
    for shift in shifts:
        shift.start()

    def window(ref, begin):
        per_t = (rows + 1) * tok
        for t in range(grid_t):
            seen = (begin <= t) & (begin + 2 >= t)
            row = jnp.where(seen, 0.0, LOW).astype(F32)
            ref[t * per_t:(t + 1) * per_t, :] = jnp.broadcast_to(row, (per_t, n_q))

    window(bias, first)
    for c in range(CORNERS_AHEAD):
        stage_corner(c)
    for side in (0, 1):
        def _(side=side):
            first_copy(1 - side).wait_recv()
            begin = jnp.concatenate(
                [first_recv[side, 0:1, col * per_col:(col + 1) * per_col] for col in columns(side, True)], axis=1)
            window(bias_z.at[side], begin)
        if_(has[side], _)

    def step(i, carry):
        def arrived():
            for shift in shifts:
                shift.wait_recv()

        if_(i + AHEAD_Y == staying, arrived)
        if_(i + AHEAD_Y < chunks, lambda: y_kv(i + AHEAD_Y).start())
        if_(i + ahead_q < chunks, lambda: queries_send(i + ahead_q))
        if_(i + ahead_e < chunks, lambda: keys_send(i + ahead_e))
        if_(i + CORNERS_AHEAD < chunks, lambda: stage_corner(i + CORNERS_AHEAD))
        if_(i < chunks, lambda: stage_first(i))
        if_((i >= MERGE_LAG) & (i < chunks + MERGE_LAG), lambda: stage_merge(i - MERGE_LAG))
        if_((i >= STAT_LAG) & (i < chunks + STAT_LAG), lambda: stage_second(i - STAT_LAG))
        if_(i >= FOLD_LAG, lambda: stage_fold(i - FOLD_LAG))
        return carry

    lax.fori_loop(0, chunks + FOLD_LAG, step, 0)
    result(slice(None), slice(None), slice(None), slice(None), slice(None), kept).wait()
    for shift in shifts:
        shift.wait_send()
    for side in (0, 1):
        if_(has[side], lambda: first_copy(side).wait_send())


def local(mesh_sizes, queries, keys_values, grad_out, time_start):
    n_sec, n_ha, n_wa = mesh_sizes
    q, kv, go = queries[0], keys_values[:, 0], grad_out[0]
    grid_t, rows, cols, tok, channels = q.shape
    assert n_ha == 2 and rows == 2 and cols == 2 and n_wa >= 4 and n_sec >= 2
    width = HEADS_PER_CHUNK * HEAD_DIM
    assert channels % width == 0
    chunks = channels // width
    assert chunks >= max(AHEAD_Y, *AHEAD_Q, *AHEAD_E) and AHEAD_Y >= CORNERS_AHEAD
    assert AHEAD_Y >= max(*AHEAD_Q, *AHEAD_E) and chunks - SHIFTED >= AHEAD_Y and SHIFTED > 0
    per_col, per_key = grid_t * rows * tok, grid_t * (rows + 1) * tok
    n_q = cols * per_col
    slots = (STAT_LAG + 1) * HEADS_PER_CHUNK
    stay = pl.BlockSpec(memory_space=pl.ANY)
    vmem = pltpu.VMEM
    out = pl.pallas_call(
        functools.partial(kernel, (n_sec, n_ha, n_wa, chunks, width)),
        out_shape=pltpu.VMEM((3,) + q.shape, BF16),
        in_specs=[pl.BlockSpec(memory_space=pltpu.SMEM), stay, stay, stay],
        out_specs=pl.BlockSpec(memory_space=pltpu.VMEM),
        scratch_shapes=[
            vmem((2,) + q.shape, BF16),
            vmem((2, grid_t, rows + 1, cols + 1, tok, channels), BF16),
            vmem((2, 2) + q.shape, BF16),
            pltpu.SemaphoreType.DMA((3,)),
            vmem((8, n_q), F32),
            vmem((2, 8, n_q), F32),
            pltpu.SemaphoreType.DMA((2, 2)),
            vmem((per_key, n_q), F32),
            vmem((2, per_key, n_q), F32),
            vmem((slots, (cols + 1) * per_key, n_q), F32),
            vmem((slots, (cols + 1) * per_key, n_q), F32),
            vmem((slots, 8, n_q), F32),
            vmem((2, slots, per_key, n_q), F32),
            vmem((2, slots, per_key, n_q), F32),
            vmem((2, slots, 8, n_q), F32),
            vmem((2, chunks, HEADS_PER_CHUNK, cols, 4, per_col), F32),
            vmem((2, chunks, HEADS_PER_CHUNK, cols, 4, per_col), F32),
            vmem((2, grid_t, rows + 1, cols, tok, width), F32),
            vmem((2,) + q.shape, BF16),
            vmem((2,) + q.shape, BF16),
            vmem((2, grid_t, rows + 1, tok, channels), BF16),
            vmem((2, grid_t, rows, tok, channels), BF16),
            vmem((2, grid_t, tok, channels), BF16),
            vmem((2, grid_t, cols, tok, channels), BF16),
            vmem((2, grid_t, cols, tok, channels), BF16),
            vmem((3,) + q.shape, BF16),
            vmem((grid_t, rows, cols, tok, width), F32),
            vmem((2, grid_t, cols, tok, width), F32),
            pltpu.SemaphoreType.DMA((KINDS, chunks)),
            pltpu.SemaphoreType.DMA((KINDS, chunks)),
        ],
        compiler_params=pltpu.CompilerParams(
            collective_id=0, has_side_effects=True, vmem_limit_bytes=VMEM_KIB * 1024
        ),
    )(time_start.transpose(1, 2, 0), q, kv, go)
    return out[:, None]


def solution(mesh):
    sizes = (mesh.shape["section"], mesh.shape["ha"], mesh.shape["wa"])
    return jax.shard_map(
        functools.partial(local, sizes),
        mesh=mesh,
        in_specs=(
            P("section", None, "ha", "wa", None, None),
            P(None, "section", None, "ha", "wa", None, None),
            P("section", None, "ha", "wa", None, None),
            P(None, "ha", "wa"),
        ),
        out_specs=P(None, "section", None, "ha", "wa", None, None),
        check_vma=False,
    )
```
